32 devices in a mesh: seq: 4 (over x, core), exp: 8 (over z, y).
Axes of the slice: x: 2, y: 2, z: 4, core: 2. Of those that a mesh axis runs over, the one named last changes fastest.
Arguments:
- query_rows: bfloat16 [8, 768, 4096], P('exp', 'seq'), may hold values from -6 to 6
- key_rows: bfloat16 [8, 768, 512], P('exp', 'seq'), may hold values from -6 to 6
- value_matrix: bfloat16 [8, 768, 512], P('exp', 'seq'), may hold values from -6 to 6
- doc_ids: int32 [8, 768], P('exp'), may hold values from 0 to 7, as said below
- out_weight: bfloat16 [4096, 2048], P(('seq', 'exp')), may hold values from -0.375 to 0.375
- enc_weight: bfloat16 [32, 2048, 1024], P(('seq', 'exp')), may hold values from -0.125 to 0.125
- enc_bias: float32 [32, 1024], P(('seq', 'exp')), may hold values from -3 to 3
- dec_weight: bfloat16 [32, 1024, 2048], P(('seq', 'exp')), may hold values from -0.1875 to 0.1875
- dec_bias: float32 [2048], replicated, may hold values from -3 to 3
- expert_ids: int32 [8, 768], P('exp', 'seq'), may hold values from 0 to 31
- slot_ids: int32 [8, 768], P('exp', 'seq'), may hold values from -1 to 11, as said below
Outputs:
- harvested: bfloat16 [8, 768, 2048], P('exp', 'seq')
- reconstruction: bfloat16 [8, 768, 2048], P('exp', 'seq')
- error_rows: bfloat16 [8, 768, 2048], P('exp', 'seq')
- dec_grad: bfloat16 [32, 1024, 2048], P(('seq', 'exp'))
The draws below stay inside these ranges and needn't reach their ends.
Inputs may be any that keep to these rules, and one draw needn't show every extreme that they name: `doc_ids`: each sequence's numbers start at 0, never fall, and rise by one at each of 7 document starts. `slot_ids`: among one device's tokens, those that name the same expert and are kept hold the slots 0 to n - 1 in some order, n at most 12; -1 marks a token left out. In every draw some expert holds all 12 slots on every device.
All inputs are finite; a program needn't handle non-finite values.
Results may differ from the reference program's by a relative error of at most 0.014.
Values may be sent and summed in bfloat16 or wider, within the bound.
No kernel may reach another device: no remote copies, remote signals or barrier semaphores. Data moves between devices by JAX's collectives and lax.ppermute only.
A program may use at most 128 MiB of HBM per device.

```python
import math
import jax
import jax.numpy as jnp
from jax import lax

D = 2048
QUERY_HEADS = 32
KEY_VALUE_HEADS = 4
HEAD_DIMENSION = 128
F = 1024
DOCS = 8
TOK_DEV = 192
SEQUENCE_LENGTH = 768
SEQUENCE_COUNT = 8
EXPERTS = 32
CAP = 12


def segment_table(key):
    sequence_keys = jax.random.split(key, SEQUENCE_COUNT)

    def one_sequence(sequence_key):
        cut_points = jax.random.permutation(sequence_key, SEQUENCE_LENGTH - 1)[:DOCS - 1] + 1
        places = jnp.arange(SEQUENCE_LENGTH)
        return jnp.sum(places[:, None] >= cut_points[None, :], axis=1).astype(jnp.int32)
    return jax.vmap(one_sequence)(sequence_keys)


def draw_query_rows(key, part):
    full_dimensions = (SEQUENCE_COUNT, SEQUENCE_LENGTH, QUERY_HEADS * HEAD_DIMENSION)
    value_output = jnp.clip(jax.random.normal(jax.random.fold_in(key, 41), full_dimensions), -6.0, 6.0)
    return value_output.astype(jnp.bfloat16)


def draw_key_rows(key, part):
    full_dimensions = (SEQUENCE_COUNT, SEQUENCE_LENGTH, KEY_VALUE_HEADS * HEAD_DIMENSION)
    value_output = jnp.clip(jax.random.normal(jax.random.fold_in(key, 43), full_dimensions), -6.0, 6.0)
    return value_output.astype(jnp.bfloat16)


def draw_doc_ids(key, part):
    return segment_table(jax.random.fold_in(key, 11))


def routing_tables(key):
    blocks = SEQUENCE_COUNT * (SEQUENCE_LENGTH // TOK_DEV)
    hot_count = CAP + max(1, CAP // 3)
    hot_expert = jax.random.randint(jax.random.fold_in(key, 1), (), 0, EXPERTS)
    relabel = jax.random.permutation(jax.random.fold_in(key, 2), EXPERTS - 1)
    first_pick = jax.random.randint(jax.random.fold_in(key, 3), (blocks, TOK_DEV), 0, EXPERTS - 1)
    second_pick = jax.random.randint(jax.random.fold_in(key, 4), (blocks, TOK_DEV), 0, EXPERTS - 1)
    others = (hot_expert + 1 + relabel[jnp.minimum(first_pick, second_pick)]) % EXPERTS
    order_keys = jax.random.split(jax.random.fold_in(key, 5), blocks)
    hot_rank = jax.vmap(lambda one_key: jax.random.permutation(one_key, TOK_DEV))(order_keys)
    chosen_expert = jnp.where(hot_rank < hot_count, hot_expert, others).astype(jnp.int32)
    slot_keys = jax.random.split(jax.random.fold_in(key, 6), blocks)
    priority = jax.vmap(lambda one_key: jax.random.permutation(one_key, TOK_DEV))(slot_keys)
    same_expert = chosen_expert[:, :, None] == chosen_expert[:, None, :]
    earlier = priority[:, None, :] < priority[:, :, None]
    ranking = jnp.sum(same_expert & earlier, axis=2)
    slot_table = jnp.where(ranking < CAP, ranking, -1).astype(jnp.int32)
    return (chosen_expert.reshape(SEQUENCE_COUNT, SEQUENCE_LENGTH), slot_table.reshape(SEQUENCE_COUNT, SEQUENCE_LENGTH))


def draw_expert_ids(key, part):
    return routing_tables(jax.random.fold_in(key, 23))[0]


def draw_slot_ids(key, part):
    return routing_tables(jax.random.fold_in(key, 23))[1]


def shard_levels(own_key, dims, pieces, smallest, largest):
    gain, own = 1.0, jax.random.fold_in(own_key, 6)
    for dim, shards_of in pieces:
        heights = jnp.exp(jax.random.uniform(jax.random.fold_in(own, dim), (shards_of,), jnp.float32, smallest / len(pieces), largest / len(pieces)))
        gain = gain * jnp.repeat(heights, dims[dim] // shards_of).reshape([-1 if axis == dim else 1 for axis in range(len(dims))])
    return gain


def normal_values(stream_key, extent, scale, bound, cuts=(), kind=jnp.bfloat16):
    values = jax.random.normal(stream_key, extent, jnp.float32) * scale
    if len(cuts) > 0:
        values = shard_levels(stream_key, extent, cuts, -0.22, 0.18) * values
    return jnp.clip(values, min=-bound, max=bound).astype(kind)


def setup_inputs(seed: int = 0) -> dict:
    splits = jax.random.split(jax.random.key(seed), 12)
    return {
        "query_rows": draw_query_rows(jax.random.fold_in(splits[11], 71), 0),
        "key_rows": draw_key_rows(jax.random.fold_in(splits[11], 71), 0),
        "value_matrix": normal_values(splits[2], (SEQUENCE_COUNT, SEQUENCE_LENGTH, KEY_VALUE_HEADS * HEAD_DIMENSION), 1.0, 6.0, ((0, 8), (1, 4))),
        "doc_ids": draw_doc_ids(jax.random.fold_in(splits[11], 71), 0),
        "out_weight": normal_values(splits[4], (QUERY_HEADS * HEAD_DIMENSION, D), (QUERY_HEADS * HEAD_DIMENSION // 16) ** -0.5, 0.375, ((0, 32),)),
        "enc_weight": normal_values(splits[5], (EXPERTS, D, F), D ** -0.5, 0.125, ((0, 32),)),
        "enc_bias": normal_values(splits[6], (EXPERTS, F), 0.5, 3.0, ((0, 32),), jnp.float32),
        "dec_weight": normal_values(splits[7], (EXPERTS, F, D), F ** -0.5, 0.1875, ((0, 32),)),
        "dec_bias": normal_values(splits[8], (D,), 0.5, 3.0, (), jnp.float32),
        "expert_ids": draw_expert_ids(jax.random.fold_in(splits[11], 71), 0),
        "slot_ids": draw_slot_ids(jax.random.fold_in(splits[11], 71), 0),
    }


masked_score = -1e+30

def attend_sequence(query_seq, key_sequence, value_sequence, doc_seq):
    span_length = query_seq.shape[0]
    query_group_width = QUERY_HEADS // KEY_VALUE_HEADS
    query_heads = query_seq.reshape(span_length, QUERY_HEADS, HEAD_DIMENSION).transpose(1, 0, 2)
    key_head_rows = key_sequence.reshape(span_length, KEY_VALUE_HEADS, HEAD_DIMENSION).transpose(1, 0, 2)
    value_head_rows = value_sequence.reshape(span_length, KEY_VALUE_HEADS, HEAD_DIMENSION).transpose(1, 0, 2)
    positions = jnp.arange(span_length, dtype=jnp.int32)
    visible = (positions[:, None] >= positions[None, :]) & (doc_seq[:, None] == doc_seq[None, :])
    score_scale = 1.0 / math.sqrt(HEAD_DIMENSION)

    def one_head(head_index):
        query_one = query_heads[head_index]
        key_one = key_head_rows[head_index // query_group_width]
        value_one = value_head_rows[head_index // query_group_width]
        scores = jnp.dot(query_one, key_one.T, preferred_element_type=jnp.float32) * score_scale
        scores = jnp.where(visible, scores, masked_score)
        highest = lax.optimization_barrier(jnp.max(scores, axis=1, keepdims=True))
        weights = jnp.exp(scores - highest)
        normed = (weights / lax.optimization_barrier(jnp.sum(weights, axis=1, keepdims=True))).astype(jnp.bfloat16)
        return jnp.dot(normed, value_one, preferred_element_type=jnp.float32).astype(jnp.bfloat16)
    mixed = lax.map(one_head, jnp.arange(QUERY_HEADS, dtype=jnp.int32))
    return mixed.transpose(1, 0, 2).reshape(span_length, QUERY_HEADS * HEAD_DIMENSION)

def reference(query_rows, key_rows, value_matrix, doc_ids, out_weight, enc_weight, enc_bias, dec_weight, dec_bias, expert_ids, slot_ids):

    def one_sequence(items):
        query_seq, key_sequence, value_sequence, doc_seq = items
        attended = attend_sequence(query_seq, key_sequence, value_sequence, doc_seq)
        return jnp.dot(attended, out_weight, preferred_element_type=jnp.float32).astype(jnp.bfloat16)
    harvested = lax.map(one_sequence, (query_rows, key_rows, value_matrix, doc_ids))
    tokens_all = SEQUENCE_COUNT * SEQUENCE_LENGTH
    flat_rows = harvested.reshape(tokens_all, D)
    flat_expert = expert_ids.reshape(tokens_all)
    flat_slot = slot_ids.reshape(tokens_all)
    kept_token = flat_slot >= 0
    token_index = jnp.arange(tokens_all, dtype=jnp.int32)
    source_block = token_index // TOK_DEV
    slot_total = tokens_all // TOK_DEV * CAP
    padded_rows = jnp.concatenate([flat_rows, jnp.zeros((1, D), jnp.bfloat16)], axis=0)

    def one_expert(rebuilt_all, expert_index):
        mine = kept_token & (flat_expert == expert_index)
        place = jnp.where(mine, source_block * CAP + flat_slot, slot_total).astype(jnp.int32)
        table = jnp.full((slot_total,), tokens_all, jnp.int32).at[place].set(token_index, mode='drop')
        slot_rows = padded_rows[table]
        slot_live = table < tokens_all
        centered = (slot_rows.astype(jnp.float32) - dec_bias).astype(jnp.bfloat16)
        pre_act = jnp.dot(centered, enc_weight[expert_index], preferred_element_type=jnp.float32) + enc_bias[expert_index]
        latent = jnp.maximum(pre_act, jnp.float32(0.0)).astype(jnp.bfloat16)
        rebuilt = (jnp.dot(latent, dec_weight[expert_index], preferred_element_type=jnp.float32) + dec_bias).astype(jnp.bfloat16)
        residue = (rebuilt.astype(jnp.float32) - slot_rows.astype(jnp.float32)).astype(jnp.bfloat16)
        gated = jnp.where(slot_live[:, None], latent, jnp.zeros_like(latent))
        grad_one = jnp.dot(gated.T, residue, preferred_element_type=jnp.float32).astype(jnp.bfloat16)
        rebuilt_all = rebuilt_all.at[table].set(rebuilt)
        return (rebuilt_all, grad_one)
    start_rows = jnp.zeros((tokens_all + 1, D), jnp.bfloat16)
    rebuilt_all, dec_grad = lax.scan(one_expert, start_rows, jnp.arange(EXPERTS, dtype=jnp.int32))
    reconstruction = jnp.where(kept_token[:, None], rebuilt_all[:tokens_all], dec_bias.astype(jnp.bfloat16)[None, :])
    error_rows = (reconstruction.astype(jnp.float32) - flat_rows.astype(jnp.float32)).astype(jnp.bfloat16)
    return (harvested, reconstruction.reshape(SEQUENCE_COUNT, SEQUENCE_LENGTH, D), error_rows.reshape(SEQUENCE_COUNT, SEQUENCE_LENGTH, D), dec_grad)
```

```python
import functools
import math

import jax
import jax.numpy as jnp
from jax import lax
from jax.experimental import pallas as pl
from jax.experimental.pallas import tpu as pltpu
from jax.sharding import PartitionSpec as P

HEAD_DIMENSION = 128
CORES = 2
KEY_BLOCK = 128
ROW_BLOCK = 64
EMPTY = 1e30
MASKED = -1e30
CHUNKS = 2

bf16 = jnp.bfloat16
f32 = jnp.float32


def call(kernel, name, out_shape, flops, moved, **kw):
    return pl.pallas_call(
        kernel,
        name=name,
        out_shape=out_shape,
        cost_estimate=pl.CostEstimate(flops=int(flops), bytes_accessed=int(moved), transcendentals=0),
        **kw,
    )


def dot(a, b, dims=((1,), (0,))):
    return lax.dot_general(a, b, (dims, ((), ())), preferred_element_type=f32)


def attention_kernel(
    heads, parts, scal, first, q_ref, mine_ref, theirs_ref, dcol_ref, drow_ref, o_ref,
    k_scr, v_scr, s_scr, m_scr, l_scr, a_scr,
):
    group = pl.program_id(0)
    tokens = q_ref.shape[0]
    width = k_scr.shape[1]
    hd = HEAD_DIMENSION

    @pl.when(group == 0)
    def _():
        for d in range(parts):
            for which, ref in enumerate((mine_ref, theirs_ref)):
                at = pl.multiple_of(scal[2 + d * CORES + which] * tokens, tokens)
                k_scr[pl.ds(at, tokens), :] = ref[d * tokens : (d + 1) * tokens, :width]
                v_scr[pl.ds(at, tokens), :] = ref[d * tokens : (d + 1) * tokens, width:]

    base = scal[0] * tokens
    lane = pl.multiple_of(group * hd, hd)
    scale = math.log2(math.e) / math.sqrt(hd)
    rows = heads * ROW_BLOCK

    def part(i, carry):
        at = pl.multiple_of(i * ROW_BLOCK, ROW_BLOCK)
        here = pl.multiple_of(base + at, ROW_BLOCK)
        q_all = q_ref[pl.ds(at, ROW_BLOCK), :]
        q = jnp.concatenate([q_all[:, h * hd : (h + 1) * hd] for h in range(heads)], axis=0)
        lo = first[scal[0] * (tokens // ROW_BLOCK) + i]
        hi = (here + ROW_BLOCK - 1) // KEY_BLOCK + 1
        row_pos = here + lax.broadcasted_iota(jnp.int32, (ROW_BLOCK, KEY_BLOCK), 0)
        lane_pos = lax.broadcasted_iota(jnp.int32, (ROW_BLOCK, KEY_BLOCK), 1)
        row_doc = drow_ref[pl.ds(here, ROW_BLOCK), :]
        m_scr[...] = jnp.full_like(m_scr, MASKED)

        def scores(j, carry):
            col = pl.multiple_of(j * KEY_BLOCK, KEY_BLOCK)
            s = dot(q, k_scr[pl.ds(col, KEY_BLOCK), pl.ds(lane, hd)], ((1,), (1,)))
            visible = (row_pos >= lane_pos + col) & (row_doc == dcol_ref[:, pl.ds(col, KEY_BLOCK)])
            s = jnp.where(visible[None], s.reshape(heads, ROW_BLOCK, KEY_BLOCK), MASKED)
            s = s.reshape(rows, KEY_BLOCK)
            s_scr[j - lo] = s
            m_scr[...] = jnp.maximum(m_scr[...], s)
            return carry

        lax.fori_loop(lo, hi, scores, 0)
        top = jnp.max(m_scr[...], axis=1, keepdims=True)
        m_scr[...] = jnp.broadcast_to(top * scale, m_scr.shape)
        l_scr[...] = jnp.zeros_like(l_scr)
        a_scr[...] = jnp.zeros_like(a_scr)

        def weigh(j, carry):
            col = pl.multiple_of(j * KEY_BLOCK, KEY_BLOCK)
            p = jnp.exp2(s_scr[j - lo] * scale - m_scr[...])
            l_scr[...] += p
            a_scr[...] += dot(p.astype(bf16), v_scr[pl.ds(col, KEY_BLOCK), pl.ds(lane, hd)])
            return carry

        lax.fori_loop(lo, hi, weigh, 0)
        out = (a_scr[...] / jnp.sum(l_scr[...], axis=1, keepdims=True)).astype(bf16)
        for h in range(heads):
            o_ref[pl.ds(at, ROW_BLOCK), h * hd : (h + 1) * hd] = out[
                h * ROW_BLOCK : (h + 1) * ROW_BLOCK
            ]
        return carry

    lax.fori_loop(0, tokens // ROW_BLOCK, part, 0)


def attend(scal, first, q, q_at, heads, mine, theirs, doc_col, doc_row, parts, tag):
    tokens = q.shape[0]
    span = doc_col.shape[1]
    width = mine.shape[1] // 2
    groups = width // HEAD_DIMENSION
    rows = heads * ROW_BLOCK
    lanes = heads * HEAD_DIMENSION
    whole = lambda *shape: pl.BlockSpec(shape, lambda g, *_: (0,) * len(shape))
    return call(
        functools.partial(attention_kernel, heads, parts),
        "attend_" + tag,
        jax.ShapeDtypeStruct((tokens, groups * lanes), bf16),
        4 * tokens * groups * lanes * span // 2,
        4 * tokens * groups * lanes + 8 * span * width,
        grid_spec=pltpu.PrefetchScalarGridSpec(
            num_scalar_prefetch=2,
            grid=(groups,),
            in_specs=[
                pl.BlockSpec((tokens, lanes), lambda g, sc, fi: (0, sc[1] * q_at + g)),
                whole(*mine.shape),
                whole(*theirs.shape),
                whole(1, span),
                whole(span, 1),
            ],
            out_specs=pl.BlockSpec((tokens, lanes), lambda g, *_: (0, g)),
            scratch_shapes=[
                pltpu.VMEM((span, width), bf16),
                pltpu.VMEM((span, width), bf16),
                pltpu.VMEM((span // KEY_BLOCK, rows, KEY_BLOCK), f32),
                pltpu.VMEM((rows, KEY_BLOCK), f32),
                pltpu.VMEM((rows, KEY_BLOCK), f32),
                pltpu.VMEM((rows, HEAD_DIMENSION), f32),
            ],
        ),
    )(scal, first, q, mine, theirs, doc_col, doc_row)


def order_kernel(order, *refs):
    blocks, out = refs[:-1], refs[-1]
    depth = blocks[0].shape[0]
    at = lambda i: pl.multiple_of(order[i] * depth, depth)
    for i, block in enumerate(blocks[:-2]):
        out[pl.ds(at(i), depth), :] = block[...]
    last = at(len(blocks) - 2)
    out[pl.ds(pl.multiple_of(last, depth // 2), depth // 2), :] = blocks[-2][...]
    out[pl.ds(pl.multiple_of(last + depth // 2, depth // 2), depth // 2), :] = blocks[-1][...]


def in_order(order, blocks):
    depth, cols = blocks[0].shape
    rows = depth * (len(blocks) - 1)
    vmem = pl.BlockSpec(memory_space=pltpu.VMEM)
    return call(
        order_kernel,
        "in_order",
        jax.ShapeDtypeStruct((rows, cols), bf16),
        0,
        4 * rows * cols,
        in_specs=[pl.BlockSpec(memory_space=pltpu.SMEM)] + [vmem] * len(blocks),
        out_specs=vmem,
    )(order, *blocks)


def ring_gather(w, ring):
    size = len(ring)
    half = size // 2
    ahead = [(ring[i], ring[(i + 1) % size]) for i in range(size)]
    back = [(ring[i], ring[(i - 1) % size]) for i in range(size)]
    depth = w.shape[0]
    fw = bw = w
    blocks = [w]
    for step in range(1, half):
        fw = lax.ppermute(fw, "exp", ahead)
        bw = lax.ppermute(bw, "exp", back)
        blocks += [fw, bw]
    blocks.append(lax.ppermute(fw[: depth // 2], "exp", ahead))
    blocks.append(lax.ppermute(bw[depth // 2 :], "exp", back))
    return blocks


def project_kernel(depth, scal, *refs):
    rest, (w_mine, w_theirs, own_ref), sends = refs[: len(refs) // 2 - 1], refs[len(refs) // 2 - 1 : len(refs) // 2 + 2], refs[len(refs) // 2 + 2 :]
    tokens = rest[0].shape[0]
    a = pl.multiple_of(scal[0] * depth, depth)
    b = pl.multiple_of((1 - scal[0]) * depth, depth)
    x = jnp.concatenate([r[:, pl.ds(a, depth)] for r in rest], axis=0)
    y = jnp.concatenate([r[:, pl.ds(b, depth)] for r in rest], axis=0)
    out = dot(x, w_mine[...]) + dot(y, w_theirs[...])
    own_ref[...] = out[:tokens]
    for i, ref in enumerate(sends):
        ref[...] = out[(i + 1) * tokens : (i + 2) * tokens].astype(bf16)


def project(core, attended, w_mine, w_theirs):
    tokens, width = attended[0].shape
    depth, cols = w_mine.shape
    parts = len(attended)
    tile = min(512, cols)
    col = lambda n: pl.BlockSpec((n, tile), lambda i, *_: (0, i))
    full = pl.BlockSpec((tokens, width), lambda i, *_: (0, 0))
    return call(
        functools.partial(project_kernel, depth),
        "project",
        [jax.ShapeDtypeStruct((tokens, cols), f32)]
        + [jax.ShapeDtypeStruct((tokens, cols), bf16)] * (parts - 1),
        2 * parts * tokens * width * cols,
        2 * parts * tokens * width + 2 * width * cols,
        grid_spec=pltpu.PrefetchScalarGridSpec(
            num_scalar_prefetch=1,
            grid=(cols // tile,),
            in_specs=[full] * parts + [col(depth)] * 2,
            out_specs=[col(tokens)] * parts,
        ),
    )(core, *attended, w_mine, w_theirs)


class Slots:
    def __init__(self, capacity, devices):
        self.devices = devices
        self.full = capacity // 8
        rest = capacity % 8
        self.tail = 0
        if rest:
            self.tail = 1
            while self.tail < rest:
                self.tail *= 2
        self.cuts = 8 // self.tail if self.tail else 0
        self.rows = 8 * devices
        self.groups = self.full + (1 if self.tail else 0)

    def width(self, cols):
        return self.full * cols + (cols // self.cuts if self.tail else 0)


def slot_keys(slots, expert, slot):
    keys = []
    kept = slot >= 0
    for g in range(slots.full):
        ok = kept & (slot >= 8 * g) & (slot < 8 * g + 8)
        keys.append(jnp.where(ok, expert * 8 + slot - 8 * g, -1))
    if slots.tail:
        rest = slot - 8 * slots.full
        for i in range(slots.cuts):
            keys.append(jnp.where(kept & (rest >= 0), expert * 8 + i * slots.tail + rest, -1))
    return jnp.stack(keys, axis=0).astype(jnp.int32)


def one_hot(keys_ref, i, rows):
    n = keys_ref.shape[1]
    return lax.broadcasted_iota(jnp.int32, (rows, n), 0) == keys_ref[i : i + 1, :]


def pack_kernel(slots, parts, keys_ref, own_ref, *refs):
    recv, (rows_ref, out_ref) = refs[:parts], refs[-2:]
    total = own_ref[...]
    for r in recv:
        total = total + r[...].astype(f32)
    x = total.astype(bf16)
    rows_ref[...] = x
    cols = x.shape[1]

    def place(hot, part):
        hot = hot.astype(f32)
        return dot(hot.astype(bf16), part), jnp.sum(hot, axis=1, keepdims=True)

    for g in range(slots.full):
        rows, live = place(one_hot(keys_ref, g, slots.rows), x)
        out_ref[:, g * cols : (g + 1) * cols] = jnp.where(live > 0, rows, EMPTY).astype(bf16)
    if slots.tail:
        cut = cols // slots.cuts
        acc = live_all = None
        for i in range(slots.cuts):
            rows, live = place(one_hot(keys_ref, slots.full + i, slots.rows), x[:, i * cut : (i + 1) * cut])
            acc = rows if acc is None else acc + rows
            live_all = live if live_all is None else live_all + live
        out_ref[:, slots.full * cols :] = jnp.where(live_all > 0, acc, EMPTY).astype(bf16)


def pack(slots, keys, own, received, rows_out, chunk):
    tokens, cols = own.shape
    width = slots.width(cols)
    parts = len(received)
    full = lambda *shape: pl.BlockSpec(shape, lambda i: (0,) * len(shape))
    args = [keys, own, *received]
    specs = [full(*a.shape) for a in args]
    alias = {}
    if rows_out.shape != (0,):
        alias = {len(args): 0}
        args.append(rows_out)
        specs.append(pl.BlockSpec(memory_space=pl.ANY))
    model = cols * CHUNKS

    def kernel(*refs):
        keep = refs[: 2 + parts] + refs[-2:]
        pack_kernel(slots, parts, *keep)

    return call(
        kernel,
        "pack",
        [
            jax.ShapeDtypeStruct((tokens, model), bf16),
            jax.ShapeDtypeStruct((slots.rows, width), bf16),
        ],
        4 * slots.rows * tokens * cols,
        8 * tokens * cols + 2 * slots.rows * width,
        grid=(1,),
        in_specs=specs,
        out_specs=[
            pl.BlockSpec((tokens, cols), lambda i: (0, chunk)),
            full(slots.rows, width),
        ],
        input_output_aliases=alias,
    )(*args)


def spread(slots, block):
    cols = block.shape[1]
    full, cuts = slots.full, slots.cuts
    n = cols * cuts // (full * cuts + 1) if slots.tail else cols // full
    out = [block[:, g * n : (g + 1) * n].astype(f32) for g in range(full)]
    if slots.tail:
        rest = block[:, full * n :].astype(f32)
        rows = rest.shape[0]
        out.append(
            jnp.concatenate(
                [rest]
                + [pltpu.roll(rest, rows - i * slots.tail, 0) for i in range(1, cuts)],
                axis=1,
            )
        )
    return out


def tail_rows(slots, shape):
    return lax.broadcasted_iota(jnp.int32, shape, 0) % 8


def encode_kernel(slots, first, last, block_ref, bias_ref, w_ref, *refs):
    refs = list(refs)
    prev_ref = None if first else refs.pop(0)
    enc_bias_ref = refs.pop(0) if last else None
    out_ref = refs.pop(0)
    n = slots.rows
    for g, rows in enumerate(spread(slots, block_ref[...])):
        live = rows[:, :1] < EMPTY / 2
        if slots.tail and g == slots.full:
            live = live & (tail_rows(slots, (n, 1)) < slots.tail)
        x = jnp.where(live, rows - bias_ref[...], 0.0).astype(bf16)
        at = slice(g * n, (g + 1) * n)
        pre = dot(x, w_ref[0])
        if prev_ref is not None:
            pre = pre + prev_ref[at]
        if last:
            pre = jnp.maximum(pre + enc_bias_ref[...], 0.0)
            pre = jnp.where(live, pre, 0.0)
        out_ref[at] = pre.astype(out_ref.dtype)


def encode(slots, block, dec_bias, enc, chunk, prev, enc_bias):
    first, last = prev is None, enc_bias is not None
    _, model, hidden = enc.shape
    cols = model // CHUNKS
    n = slots.rows * slots.groups
    full = lambda *shape: pl.BlockSpec(shape, lambda i: (0,) * len(shape))
    args = [block, dec_bias, enc]
    specs = [
        full(*block.shape),
        pl.BlockSpec((1, cols), lambda i: (0, chunk)),
        pl.BlockSpec((1, cols, hidden), lambda i: (0, chunk, 0)),
    ]
    for extra in (prev, enc_bias):
        if extra is not None:
            args.append(extra)
            specs.append(full(*extra.shape))
    return call(
        functools.partial(encode_kernel, slots, first, last),
        "encode",
        jax.ShapeDtypeStruct((n, hidden), bf16 if last else f32),
        2 * n * cols * hidden,
        2 * cols * hidden + 2 * block.size + 4 * n * hidden,
        grid=(1,),
        in_specs=specs,
        out_specs=full(n, hidden),
    )(*args)


def decode_kernel(slots, latent_ref, w_ref, bias_ref, block_ref, out_ref, residue_ref):
    n = slots.rows
    source = spread(slots, block_ref[...])
    cols = w_ref.shape[2]
    for g in range(slots.groups):
        at = slice(g * n, (g + 1) * n)
        rebuilt = (dot(latent_ref[at], w_ref[0]) + bias_ref[...]).astype(bf16).astype(f32)
        tail = slots.tail and g == slots.full
        live = source[g][:, :1] < EMPTY / 2
        if tail:
            live = live & (tail_rows(slots, (n, 1)) < slots.tail)
        residue_ref[at] = jnp.where(live, rebuilt - source[g], 0.0).astype(bf16)
        if not tail:
            out_ref[:, g * cols : (g + 1) * cols] = rebuilt.astype(bf16)
            continue
        cut = cols // slots.cuts
        rest = rebuilt[:, :cut]
        which = tail_rows(slots, (n, 1)) // slots.tail
        for i in range(1, slots.cuts):
            moved = pltpu.roll(rebuilt[:, i * cut : (i + 1) * cut], i * slots.tail, 0)
            rest = jnp.where(which == i, moved, rest)
        out_ref[:, slots.full * cols :] = rest.astype(bf16)


def decode(slots, latent, dec, dec_bias, block, chunk):
    _, hidden, model = dec.shape
    cols = model // CHUNKS
    n = latent.shape[0]
    full = lambda *shape: pl.BlockSpec(shape, lambda i: (0,) * len(shape))
    return call(
        functools.partial(decode_kernel, slots),
        "decode",
        [
            jax.ShapeDtypeStruct(block.shape, bf16),
            jax.ShapeDtypeStruct((n, cols), bf16),
        ],
        2 * n * cols * hidden,
        2 * cols * hidden + 4 * block.size + 2 * n * hidden + 2 * n * cols,
        grid=(1,),
        in_specs=[
            full(n, hidden),
            pl.BlockSpec((1, hidden, cols), lambda i: (0, 0, chunk)),
            pl.BlockSpec((1, cols), lambda i: (0, chunk)),
            full(*block.shape),
        ],
        out_specs=[full(*block.shape), full(n, cols)],
    )(latent, dec, dec_bias, block)


def grad_kernel(latent_ref, *refs):
    residues, out_ref = refs[:-1], refs[-1]
    cols = residues[0].shape[1]
    for j, r in enumerate(residues):
        out_ref[0, :, j * cols : (j + 1) * cols] = dot(
            latent_ref[...], r[...], ((0,), (0,))
        ).astype(bf16)


def decoder_grad(latent, residues):
    n, hidden = latent.shape
    cols = residues[0].shape[1]
    model = cols * len(residues)
    tile = min(256, hidden)
    return call(
        grad_kernel,
        "decoder_grad",
        jax.ShapeDtypeStruct((1, hidden, model), bf16),
        2 * n * hidden * model,
        2 * hidden * model + 2 * n * (hidden + model),
        grid=(hidden // tile,),
        in_specs=[pl.BlockSpec((n, tile), lambda i: (0, i))]
        + [pl.BlockSpec((n, cols), lambda i: (0, 0))] * len(residues),
        out_specs=pl.BlockSpec((1, tile, model), lambda i: (0, i, 0)),
    )(latent, *residues)


def finish_kernel(slots, keys_ref, kept_ref, block_ref, bias_ref, rows_ref, *refs):
    recon_ref, error_ref = refs[-2:]
    cols = rows_ref.shape[1]
    turn = lambda i, part: dot(
        one_hot(keys_ref, i, slots.rows).astype(f32).astype(bf16), part, ((0,), (0,))
    )
    total = 0.0
    for g in range(slots.full):
        total = total + turn(g, block_ref[:, g * cols : (g + 1) * cols])
    if slots.tail:
        rest = block_ref[:, slots.full * cols :]
        total = total + jnp.concatenate(
            [turn(slots.full + i, rest) for i in range(slots.cuts)], axis=1
        )
    recon = jnp.where(kept_ref[...] > 0, total, bias_ref[...]).astype(bf16)
    recon_ref[...] = recon
    error_ref[...] = (recon.astype(f32) - rows_ref[...].astype(f32)).astype(bf16)


def finish(slots, keys, kept, block, dec_bias, rows, chunk, outs):
    tokens, model = rows.shape
    cols = model // CHUNKS
    full = lambda *shape: pl.BlockSpec(shape, lambda i: (0,) * len(shape))
    col = lambda n: pl.BlockSpec((n, cols), lambda i: (0, chunk))
    args = [keys, kept, block, dec_bias, rows]
    specs = [full(*keys.shape), full(*kept.shape), full(*block.shape), col(1), col(tokens)]
    alias = {}
    if outs:
        alias = {len(args): 0, len(args) + 1: 1}
        args += list(outs)
        specs += [pl.BlockSpec(memory_space=pl.ANY)] * 2
    return call(
        functools.partial(finish_kernel, slots),
        "finish",
        [jax.ShapeDtypeStruct((tokens, model), bf16)] * 2,
        4 * slots.rows * tokens * cols,
        6 * tokens * cols + 2 * block.size,
        grid=(1,),
        in_specs=specs,
        out_specs=[col(tokens)] * 2,
        input_output_aliases=alias,
    )(*args)


def shards(
    query_rows,
    key_rows,
    value_matrix,
    doc_ids,
    out_weight,
    enc_weight,
    enc_bias,
    dec_weight,
    dec_bias,
    expert_ids,
    slot_ids,
):
    q, k, v = query_rows[0], key_rows[0], value_matrix[0]
    tokens = q.shape[0]
    size, exp_size = lax.axis_size("seq"), lax.axis_size("exp")
    chips = size // CORES
    devices = size * exp_size
    me = lax.axis_index("seq")
    chip, core = me // CORES, me % CORES
    q_cols, kv_cols = q.shape[1] // chips, k.shape[1] // chips
    heads = q.shape[1] // k.shape[1]
    span = tokens * size
    model = out_weight.shape[1]
    cols = model // CHUNKS

    def over(d):
        return [
            (a * CORES + b, ((a + d) % chips) * CORES + b)
            for a in range(chips)
            for b in range(CORES)
        ]

    swap = [(a, a ^ 1) for a in range(size)]

    def cut(x, at, n):
        return lax.dynamic_slice(x, (0, at * n), (x.shape[0], n))

    pair = lambda at: jnp.concatenate([cut(k, at, kv_cols), cut(v, at, kv_cols)], axis=1)
    kv_parts = [pair(chip)]
    q_parts = [q]
    for d in range(1, chips):
        to = (chip + d) % chips
        kv_parts.append(lax.ppermute(pair(to), "seq", over(d)))
        q_parts.append(lax.ppermute(cut(q, to, q_cols), "seq", over(d)))
    mine = jnp.concatenate(kv_parts, axis=0)
    theirs = lax.ppermute(mine, "seq", swap)

    ring = [2 * i for i in range(exp_size // 2)] + [2 * i + 1 for i in reversed(range(exp_size // 2))]
    exp_me = lax.axis_index("exp")
    place = jnp.where(exp_me % 2 == 0, exp_me // 2, exp_size - 1 - exp_me // 2)
    offsets = [0]
    for step in range(1, exp_size // 2):
        offsets += [-step, step]
    offsets.append(exp_size // 2)
    spot = (place + jnp.array(offsets, jnp.int32)) % exp_size
    order = jnp.where(
        spot < exp_size // 2, 2 * spot, 2 * (exp_size - 1 - spot) + 1
    ).astype(jnp.int32)
    w_mine, w_theirs = [], []
    for j in range(CHUNKS):
        got = in_order(order, ring_gather(out_weight[:, j * cols : (j + 1) * cols], ring))
        w_mine.append(got)
        w_theirs.append(lax.ppermute(got, "seq", swap))

    doc_col = doc_ids
    doc_row = doc_ids.reshape(span, 1)
    starts = jnp.sum(
        (doc_ids < doc_ids[0, ::ROW_BLOCK][:, None]).astype(jnp.int32), axis=1
    ) // KEY_BLOCK
    attended = []
    for d in range(chips):
        seats = []
        for a in range(chips):
            seats += [((chip - a) % chips) * CORES + core, ((chip - a) % chips) * CORES + 1 - core]
        scal = jnp.stack([seats[d * CORES], chip if d == 0 else 0 * chip] + seats).astype(jnp.int32)
        attended.append(
            attend(
                scal,
                starts,
                q_parts[d],
                q_cols // (heads * HEAD_DIMENSION),
                heads,
                mine,
                theirs,
                doc_col,
                doc_row,
                chips,
                "own" if d == 0 else "far",
            )
        )

    capacity = 2 * tokens // devices
    slots = Slots(capacity, devices)
    keys = slot_keys(slots, expert_ids[0], slot_ids[0])
    kept = (slot_ids[0] >= 0).astype(jnp.int32).reshape(tokens, 1)
    bias_row = dec_bias[None]
    core_row = core.reshape(1).astype(jnp.int32)
    rows = jnp.zeros((0,), bf16)
    arrived, sums = [], None
    to_all = lambda block: lax.all_to_all(
        block.reshape(devices, 8, block.shape[1]), ("seq", "exp"), 0, 0, tiled=True
    ).reshape(block.shape)
    for j in range(CHUNKS):
        own, *sends = project(core_row, attended, w_mine[j], w_theirs[j])
        received = [
            lax.ppermute(part, "seq", over(chips - d)) for d, part in enumerate(sends, start=1)
        ]
        rows, packed = pack(slots, keys, own, received, rows, j)
        arrived.append(to_all(packed))

    pre = None
    for j in range(CHUNKS):
        last = j == CHUNKS - 1
        pre = encode(slots, arrived[j], bias_row, enc_weight, j, pre, enc_bias if last else None)
    latent = pre
    residues, returned = [], []
    for j in range(CHUNKS):
        rebuilt, residue = decode(slots, latent, dec_weight, bias_row, arrived[j], j)
        residues.append(residue)
        returned.append(to_all(rebuilt))
    dec_grad = decoder_grad(latent, residues)
    outs = ()
    for j in range(CHUNKS):
        outs = finish(slots, keys, kept, returned[j], bias_row, rows, j, outs)
    return (rows[None], outs[0][None], outs[1][None], dec_grad)


def solution(mesh):
    return jax.shard_map(
        shards,
        mesh=mesh,
        in_specs=(
            P("exp", "seq", None),
            P("exp", "seq", None),
            P("exp", "seq", None),
            P("exp", None),
            P(("seq", "exp"), None),
            P(("seq", "exp"), None, None),
            P(("seq", "exp"), None),
            P(("seq", "exp"), None, None),
            P(),
            P("exp", "seq"),
            P("exp", "seq"),
        ),
        out_specs=(
            P("exp", "seq", None),
            P("exp", "seq", None),
            P("exp", "seq", None),
            P(("seq", "exp"), None, None),
        ),
        check_vma=False,
    )
```

```python
import functools
import math

import jax
import jax.numpy as jnp
from jax import lax
from jax.experimental import pallas as pl
from jax.experimental.pallas import tpu as pltpu
from jax.sharding import PartitionSpec as P


HEAD_DIMENSION = 128
CORES = 2
KEY_BLOCK = 256
KEY_STEP = 128
ROW_BLOCK = 64
EMPTY = 1e30
MASKED = -1e30
CHUNKS = 2
LIMIT = 20 * 2**20
ALMOST_ALL = 61_400_000
VMEM, SMEM, ANY, HBM = pltpu.VMEM, pltpu.SMEM, pl.ANY, pltpu.HBM
TILES = 4

bf16 = jnp.bfloat16
f32 = jnp.float32


def call(kernel, out_shape, flops, moved, ins, outs, scratch=(), alias={}, limit=None):
    spec = lambda space: pl.BlockSpec(memory_space=space)
    return pl.pallas_call(
        kernel,
        out_shape=out_shape,
        in_specs=[spec(s) for s in ins],
        out_specs=jax.tree.map(spec, outs),
        scratch_shapes=list(scratch),
        input_output_aliases=alias,
        cost_estimate=pl.CostEstimate(flops=int(flops), bytes_accessed=int(moved), transcendentals=0),
        compiler_params=pltpu.CompilerParams(vmem_limit_bytes=limit or LIMIT),
    )


def dot(a, b, dims=((1,), (0,))):
    return lax.dot_general(a, b, (dims, ((), ())), preferred_element_type=f32)


def attention_kernel(
    heads, parts, group, scal, first, q_ref, mine_ref, theirs_ref, dcol_ref, drow_ref, o_ref,
    k_scr, v_scr, m_scr, l_scr, a_scr,
):
    tokens = q_ref.shape[0]
    hd = HEAD_DIMENSION
    width = mine_ref.shape[1] // 2
    span = parts * CORES * tokens
    key_at = slice(group * hd, (group + 1) * hd)
    value_at = slice(width + group * hd, width + (group + 1) * hd)
    for d in range(parts):
        for which, ref in enumerate((mine_ref, theirs_ref)):
            at = pl.multiple_of(scal[2 + d * CORES + which] * tokens, tokens)
            k_scr[pl.ds(at, tokens), :] = ref[d * tokens : (d + 1) * tokens, key_at]
            v_scr[pl.ds(at, tokens), :] = ref[d * tokens : (d + 1) * tokens, value_at]
    k_scr[span:, :] = jnp.zeros((KEY_BLOCK, hd), bf16)
    v_scr[span:, :] = jnp.zeros((KEY_BLOCK, hd), bf16)

    base = scal[0] * tokens
    scale = math.log2(math.e) / math.sqrt(hd)
    rows = heads * ROW_BLOCK
    blocks = tokens // ROW_BLOCK
    lane_pos = lax.broadcasted_iota(jnp.int32, (ROW_BLOCK, KEY_BLOCK), 1)
    row_in = lax.broadcasted_iota(jnp.int32, (ROW_BLOCK, KEY_BLOCK), 0)

    def queries(i):
        at = slice(i * ROW_BLOCK, (i + 1) * ROW_BLOCK)
        lane = [pl.multiple_of(scal[1] + (group * heads + h) * hd, hd) for h in range(heads)]
        return jnp.concatenate([q_ref[at, pl.ds(n, hd)] for n in lane], axis=0)

    def scores(i, q, col):
        col = pl.multiple_of(col, KEY_STEP)
        here = pl.multiple_of(base + i * ROW_BLOCK, ROW_BLOCK)
        s = dot(q, k_scr[pl.ds(col, KEY_BLOCK), :], ((1,), (1,))) * scale
        visible = (row_in + here >= lane_pos + col) & (
            drow_ref[pl.ds(here, ROW_BLOCK), :] == dcol_ref[:, pl.ds(col, KEY_BLOCK)]
        )
        s = jnp.where(visible[None], s.reshape(heads, ROW_BLOCK, KEY_BLOCK), MASKED)
        return s.reshape(rows, KEY_BLOCK)

    def values(col):
        return v_scr[pl.ds(pl.multiple_of(col, KEY_STEP), KEY_BLOCK), :]

    starts = [first[scal[0] * blocks + i] * KEY_STEP for i in range(blocks)]
    for i in range(blocks):
        s = scores(i, queries(i), starts[i])
        top = jnp.max(s, axis=1, keepdims=True)
        p = jnp.exp2(s - top)
        m_scr[i] = top
        l_scr[i] = jnp.sum(p, axis=1, keepdims=True)
        a_scr[i] = dot(p.astype(bf16), values(starts[i]))

    for i in range(blocks):
        trips = (base + (i + 1) * ROW_BLOCK - starts[i] + KEY_BLOCK - 1) // KEY_BLOCK

        def more(j, carry):
            col = starts[i] + j * KEY_BLOCK
            s = scores(i, queries(i), col)
            old = m_scr[i]
            top = jnp.maximum(old, jnp.max(s, axis=1, keepdims=True))
            p = jnp.exp2(s - top)
            fade = jnp.exp2(old - top)
            m_scr[i] = top
            l_scr[i] = l_scr[i] * fade + jnp.sum(p, axis=1, keepdims=True)
            a_scr[i] = a_scr[i] * fade + dot(p.astype(bf16), values(col))
            return carry

        lax.fori_loop(1, trips, more, 0)

    for i in range(blocks):
        out = (a_scr[i] * (1.0 / l_scr[i])).astype(bf16)
        for h in range(heads):
            o_ref[i * ROW_BLOCK : (i + 1) * ROW_BLOCK, h * hd : (h + 1) * hd] = out[
                h * ROW_BLOCK : (h + 1) * ROW_BLOCK
            ]


def attend(scal, first, q, heads, group, mine, theirs, doc_col, doc_row, parts):
    tokens = q.shape[0]
    span = parts * CORES * tokens
    rows = heads * ROW_BLOCK
    lanes = heads * HEAD_DIMENSION
    blocks = tokens // ROW_BLOCK
    keys = pltpu.VMEM((span + KEY_BLOCK, HEAD_DIMENSION), bf16)
    column = pltpu.VMEM((blocks, rows, 1), f32)
    return call(
        functools.partial(attention_kernel, heads, parts, group),
        jax.ShapeDtypeStruct((tokens, lanes), bf16),
        4 * tokens * lanes * span // 2,
        4 * tokens * lanes + 8 * span * HEAD_DIMENSION,
        [SMEM, SMEM] + [VMEM] * 5,
        VMEM,
        [keys, keys, column, column, pltpu.VMEM((blocks, rows, HEAD_DIMENSION), f32)],
    )(scal, first, q, mine, theirs, doc_col, doc_row)


def ring_gather(w, ring, swap, flip):
    size = len(ring)
    half = size // 2
    ahead = [(ring[i], ring[(i + 1) % size]) for i in range(size)]
    back = [(ring[i], ring[(i - 1) % size]) for i in range(size)]
    fw = bw = w
    blocks = [w]
    for step in range(1, half + 1):
        if step < half or not flip:
            fw = lax.ppermute(fw, "exp", ahead)
            blocks.append(fw)
        if step < half or flip:
            bw = lax.ppermute(bw, "exp", back)
            blocks.append(bw)
    theirs = [lax.ppermute(b, "seq", swap) for b in blocks]
    return blocks, theirs


def project_far_kernel(blocks, pieces, parts, order, *refs):
    w_refs, refs = refs[: 2 * blocks], refs[2 * blocks :]
    att, refs = refs[: parts * pieces], refs[parts * pieces :]
    w_out, sends = refs[0], refs[1:]
    for which in range(2):
        for i in range(blocks):
            ref = w_refs[which * blocks + i]
            n = ref.shape[0]
            at = pl.multiple_of(order[which * blocks + i], n)
            w_out[pl.ds(at, n), :] = ref[...]
    for d, send in enumerate(sends):
        x = jnp.concatenate([r[...] for r in att[d * pieces : (d + 1) * pieces]], axis=1)
        send[...] = dot(x, w_out[...]).astype(bf16)


def project_far(order, mine, theirs, attended):
    tokens = attended[0][0].shape[0]
    pieces = len(attended[0])
    width = sum(a.shape[1] for a in attended[0])
    cols = mine[0].shape[1]
    parts = len(attended)
    flat = [a for group in attended for a in group]
    return call(
        functools.partial(project_far_kernel, len(mine), pieces, parts),
        [jax.ShapeDtypeStruct((width, cols), bf16)]
        + [jax.ShapeDtypeStruct((tokens, cols), bf16)] * parts,
        2 * parts * tokens * width * cols,
        2 * parts * tokens * width + 4 * width * cols,
        [SMEM] + [VMEM] * (2 * len(mine) + len(flat)),
        [VMEM] * (1 + parts),
    )(order, *mine, *theirs, *flat)


def project_own_kernel(*refs):
    att, (w_ref, out_ref) = refs[:-2], refs[-2:]
    out_ref[...] = dot(jnp.concatenate([r[...] for r in att], axis=1), w_ref[...])


def project_own(attended, w):
    tokens = attended[0].shape[0]
    width, cols = w.shape
    return call(
        project_own_kernel,
        jax.ShapeDtypeStruct((tokens, cols), f32),
        2 * tokens * width * cols,
        2 * tokens * width + 2 * width * cols,
        [VMEM] * (len(attended) + 1),
        VMEM,
    )(*attended, w)


class Slots:
    def __init__(self, capacity, devices):
        self.full = capacity // 8
        rest = capacity % 8
        self.tail = 0
        if rest:
            self.tail = 1
            while self.tail < rest:
                self.tail *= 2
        self.cuts = 8 // self.tail if self.tail else 0
        self.rows = 8 * devices
        self.groups = self.full + (1 if self.tail else 0)

    def width(self, cols):
        return self.full * cols + (cols // self.cuts if self.tail else 0)


def slot_keys(slots, expert, slot):
    keys = []
    kept = slot >= 0
    for g in range(slots.full):
        ok = kept & (slot >= 8 * g) & (slot < 8 * g + 8)
        keys.append(jnp.where(ok, expert * 8 + slot - 8 * g, -1))
    if slots.tail:
        rest = slot - 8 * slots.full
        for i in range(slots.cuts):
            keys.append(jnp.where(kept & (rest >= 0), expert * 8 + i * slots.tail + rest, -1))
    return jnp.stack(keys, axis=0).astype(jnp.int32)


def one_hot(keys_ref, i, rows):
    n = keys_ref.shape[1]
    return lax.broadcasted_iota(jnp.int32, (rows, n), 0) == keys_ref[i : i + 1, :]


def send(group, cols, src, dst, sems):
    at = slice(group * cols, min((group + 1) * cols, src.shape[1]))
    copy = pltpu.make_async_copy(src.at[:, at], dst.at[:, at], sems.at[group])
    copy.start()
    return copy


def pack_kernel(slots, parts, chunk, keys_ref, own_ref, *refs):
    recv, (packed_ref, rows_ref, x_ref, out_ref, sem, out_sem) = refs[:parts], refs[-6:]
    total = own_ref[...]
    for r in recv:
        total = total + r[...].astype(f32)
    x = total.astype(bf16)
    x_ref[...] = x
    cols = x.shape[1]
    copy = pltpu.make_async_copy(x_ref, rows_ref.at[:, chunk * cols : (chunk + 1) * cols], sem)
    copy.start()

    sent = []

    def place(hot, part):
        hot = hot.astype(f32)
        return dot(hot.astype(bf16), part), jnp.sum(hot, axis=1, keepdims=True)

    for g in range(slots.full):
        rows, live = place(one_hot(keys_ref, g, slots.rows), x)
        out_ref[:, g * cols : (g + 1) * cols] = jnp.where(live > 0, rows, EMPTY).astype(bf16)
        sent.append(send(g, cols, out_ref, packed_ref, out_sem))
    if slots.tail:
        cut = cols // slots.cuts
        acc = live_all = None
        for i in range(slots.cuts):
            rows, live = place(one_hot(keys_ref, slots.full + i, slots.rows), x[:, i * cut : (i + 1) * cut])
            acc = rows if acc is None else acc + rows
            live_all = live if live_all is None else live_all + live
        out_ref[:, slots.full * cols :] = jnp.where(live_all > 0, acc, EMPTY).astype(bf16)
        sent.append(send(slots.full, cols, out_ref, packed_ref, out_sem))
    copy.wait()
    for part in sent:
        part.wait()


def pack(slots, keys, own, received, rows_out, chunk):
    tokens, cols = own.shape
    width = slots.width(cols)
    parts = len(received)
    args = [keys, own, *received]
    ins = [VMEM] * len(args)
    alias = {}
    if rows_out is not None:
        alias = {len(args): 1}
        args.append(rows_out)
        ins.append(ANY)
    return call(
        functools.partial(pack_kernel, slots, parts, chunk),
        [
            jax.ShapeDtypeStruct((slots.rows, width), bf16),
            jax.ShapeDtypeStruct((tokens, cols * CHUNKS), bf16),
        ],
        4 * slots.rows * tokens * cols,
        8 * tokens * cols + 2 * slots.rows * width,
        ins,
        [HBM, ANY],
        [
            pltpu.VMEM((tokens, cols), bf16),
            pltpu.VMEM((slots.rows, width), bf16),
            pltpu.SemaphoreType.DMA,
            pltpu.SemaphoreType.DMA((slots.groups,)),
        ],
        alias,
    )(*args)


def spread(slots, block):
    cols = block.shape[1]
    full, cuts = slots.full, slots.cuts
    n = cols * cuts // (full * cuts + 1) if slots.tail else cols // full
    out = [block[:, g * n : (g + 1) * n].astype(f32) for g in range(full)]
    if slots.tail:
        rest = block[:, full * n :].astype(f32)
        rows = rest.shape[0]
        out.append(
            jnp.concatenate(
                [rest]
                + [pltpu.roll(rest, rows - i * slots.tail, 0) for i in range(1, cuts)],
                axis=1,
            )
        )
    return out


def tail_rows(shape):
    return lax.broadcasted_iota(jnp.int32, shape, 0) % 8


def live_rows(slots, groups):
    out = []
    for g, rows in enumerate(groups):
        live = rows[:, :1] < EMPTY / 2
        if slots.tail and g == slots.full:
            live = live & (tail_rows(live.shape) < slots.tail)
        out.append(live)
    return out


def row_tiles(ref, scr, sems, start):
    n = scr.shape[0] // TILES
    copies = []
    for t in range(TILES):
        copies.append(
            pltpu.make_async_copy(
                ref.at[start + t * n : start + (t + 1) * n], scr.at[t * n : (t + 1) * n], sems.at[t]
            )
        )
        copies[-1].start()
    return copies


def centered_rows(slots, block_ref, bias):
    groups = spread(slots, block_ref[...])
    live = live_rows(slots, groups)
    rows = [jnp.where(a, r - bias, 0.0).astype(bf16) for a, r in zip(live, groups)]
    return jnp.concatenate(rows, axis=0), live


def times(x, w_scr, copies, sum_scr):
    n = w_scr.shape[0] // len(copies)
    for t, copy in enumerate(copies):
        copy.wait()
        at = slice(t * n, (t + 1) * n)
        sum_scr[...] += dot(x[:, at], w_scr[at])


def encode_kernel(slots, block_ref, bias_ref, w_ref, out_ref, kept_ref, w_scr, o_scr, sems, kept_sem, out_sem):
    cols = w_scr.shape[0]
    copies = row_tiles(w_ref.at[0], w_scr, sems, 0)
    kept = pltpu.make_async_copy(block_ref, kept_ref, kept_sem)
    kept.start()
    x, _ = centered_rows(slots, block_ref, bias_ref[:, :cols])
    o_scr[...] = jnp.zeros_like(o_scr)
    times(x, w_scr, copies, o_scr)
    out = pltpu.make_async_copy(o_scr, out_ref, out_sem)
    out.start()
    kept.wait()
    out.wait()


def encode(slots, block, dec_bias, enc, cols):
    hidden = enc.shape[2]
    n = slots.rows * slots.groups
    one = pltpu.SemaphoreType.DMA
    return call(
        functools.partial(encode_kernel, slots),
        [jax.ShapeDtypeStruct((n, hidden), f32), jax.ShapeDtypeStruct(block.shape, bf16)],
        2 * n * cols * hidden,
        2 * cols * hidden + 2 * block.size + 4 * n * hidden,
        [VMEM, VMEM, HBM],
        [HBM, HBM],
        [
            pltpu.VMEM((cols, hidden), bf16),
            pltpu.VMEM((n, hidden), f32),
            pltpu.SemaphoreType.DMA((TILES,)),
            one,
            one,
        ],
        limit=ALMOST_ALL,
    )(block, dec_bias, enc)


def middle_kernel(
    slots, block_ref, bias_ref, enc_bias_ref, enc_ref, prev_ref, dec_ref,
    latent_out, packed_ref, kept_ref,
    e_scr, d_scr, p_scr, latent_scr, pack_scr, e_sems, d_sems, p_sem, kept_sem, latent_sem, sems,
):
    cols = e_scr.shape[0]
    _, model = d_scr.shape
    prev = pltpu.make_async_copy(prev_ref, p_scr, p_sem)
    prev.start()
    e_copies = row_tiles(enc_ref.at[0], e_scr, e_sems, model - cols)
    cuts = slots.cuts or 2
    cut = model // cuts
    d_copies = []
    for t in range(cuts):
        at = slice(t * cut, (t + 1) * cut)
        d_copies.append(
            pltpu.make_async_copy(dec_ref.at[0, :, at], d_scr.at[:, at], d_sems.at[t])
        )
        d_copies[-1].start()
    kept = pltpu.make_async_copy(block_ref, kept_ref, kept_sem)
    kept.start()
    x, live = centered_rows(slots, block_ref, bias_ref[:, model - cols :])
    n = slots.rows
    prev.wait()
    times(x, e_scr, e_copies, p_scr)
    for g, a in enumerate(live):
        rows = slice(g * n, (g + 1) * n)
        pre = jnp.maximum(p_scr[rows] + enc_bias_ref[...], 0.0)
        latent_scr[rows] = jnp.where(a, pre, 0.0).astype(bf16)
    latent = pltpu.make_async_copy(latent_scr, latent_out, latent_sem)
    latent.start()
    sent = []
    rest = None
    which = tail_rows((n, 1)) // slots.tail if slots.tail else None
    for t in range(cuts):
        at = slice(t * cut, (t + 1) * cut)
        d_copies[t].wait()
        out = dot(latent_scr[...], d_scr[:, at]) + bias_ref[:, at]
        for g in range(slots.full):
            here = slice(g * model + at.start, g * model + at.stop)
            pack_scr[:, here] = out[g * n : (g + 1) * n].astype(bf16)
            sent.append(
                pltpu.make_async_copy(
                    pack_scr.at[:, here], packed_ref.at[:, here], sems.at[len(sent)]
                )
            )
            sent[-1].start()
        if slots.tail:
            part = out[slots.full * n :]
            rest = part if t == 0 else jnp.where(which == t, pltpu.roll(part, t * slots.tail, 0), rest)
    if slots.tail:
        here = slice(slots.full * model, slots.full * model + cut)
        pack_scr[:, here] = rest.astype(bf16)
        sent.append(
            pltpu.make_async_copy(pack_scr.at[:, here], packed_ref.at[:, here], sems.at[len(sent)])
        )
        sent[-1].start()
    kept.wait()
    latent.wait()
    for one in sent:
        one.wait()


def middle(slots, block, dec_bias, enc_bias, enc, prev, dec, cols):
    _, model, hidden = enc.shape
    n = slots.rows * slots.groups
    out = (slots.rows, slots.width(model))
    one = pltpu.SemaphoreType.DMA
    cuts = slots.cuts or 2
    return call(
        functools.partial(middle_kernel, slots),
        [
            jax.ShapeDtypeStruct((n, hidden), bf16),
            jax.ShapeDtypeStruct(out, bf16),
            jax.ShapeDtypeStruct(block.shape, bf16),
        ],
        2 * n * (cols + model) * hidden,
        2 * (cols + model) * hidden + 6 * block.size + 6 * n * hidden,
        [VMEM] * 3 + [HBM] * 3,
        [HBM] * 3,
        [
            pltpu.VMEM((cols, hidden), bf16),
            pltpu.VMEM((hidden, model), bf16),
            pltpu.VMEM((n, hidden), f32),
            pltpu.VMEM((n, hidden), bf16),
            pltpu.VMEM(out, bf16),
            pltpu.SemaphoreType.DMA((TILES,)),
            pltpu.SemaphoreType.DMA((cuts,)),
            one, one, one,
            pltpu.SemaphoreType.DMA((slots.full * cuts + 1,)),
        ],
        limit=ALMOST_ALL,
    )(block, dec_bias, enc_bias, enc, prev, dec)


def grad_kernel(slots, latent_ref, built_ref, *refs):
    *arrived, out_ref, scr, sems = refs
    cols = scr.shape[2]
    built = spread(slots, built_ref[...])
    copies = []
    for j, block_ref in enumerate(arrived):
        at = slice(j * cols, (j + 1) * cols)
        groups = spread(slots, block_ref[...])
        residue = jnp.concatenate(
            [
                jnp.where(a, r[:, at] - rows, 0.0).astype(bf16)
                for a, r, rows in zip(live_rows(slots, groups), built, groups)
            ],
            axis=0,
        )
        scr[j] = dot(latent_ref[...], residue, ((0,), (0,))).astype(bf16)
        copies.append(pltpu.make_async_copy(scr.at[j], out_ref.at[0, :, at], sems.at[j]))
        copies[-1].start()
    for copy in copies:
        copy.wait()


def decoder_grad(slots, latent, rebuilt, arrived, model):
    n, hidden = latent.shape
    parts = len(arrived)
    return call(
        functools.partial(grad_kernel, slots),
        jax.ShapeDtypeStruct((1, hidden, model), bf16),
        2 * n * hidden * model,
        2 * hidden * model + 2 * n * (hidden + model),
        [VMEM] * (2 + parts),
        ANY,
        [pltpu.VMEM((parts, hidden, model // parts), bf16), pltpu.SemaphoreType.DMA((parts,))],
    )(latent, rebuilt, *arrived)


def finish_kernel(
    slots, keys_ref, kept_ref, block_ref, bias_ref, rows_ref, recon_out, error_out,
    recon_scr, error_scr, rows_scr, sems, rows_sem,
):
    came = pltpu.make_async_copy(rows_ref, rows_scr, rows_sem)
    came.start()
    model = rows_scr.shape[1]
    cuts = slots.cuts or 2
    cut = model // cuts
    hot = [
        one_hot(keys_ref, i, slots.rows).astype(f32).astype(bf16)
        for i in range(keys_ref.shape[0])
    ]
    turn = lambda i, part: dot(hot[i], part, ((0,), (0,)))
    copies = []
    for t in range(cuts):
        at = slice(t * cut, (t + 1) * cut)
        total = 0.0
        for g in range(slots.full):
            total = total + turn(g, block_ref[:, g * model + at.start : g * model + at.stop])
        if slots.tail:
            total = total + turn(slots.full + t, block_ref[:, slots.full * model :])
        recon = jnp.where(kept_ref[...] > 0, total, bias_ref[:, at]).astype(bf16)
        recon_scr[:, at] = recon
        if t == 0:
            came.wait()
        error_scr[:, at] = (recon.astype(f32) - rows_scr[:, at].astype(f32)).astype(bf16)
        for k, (scr, out) in enumerate(((recon_scr, recon_out), (error_scr, error_out))):
            copies.append(pltpu.make_async_copy(scr.at[:, at], out.at[:, at], sems.at[t, k]))
            copies[-1].start()
    for copy in copies:
        copy.wait()


def finish(slots, keys, kept, block, dec_bias, rows):
    tokens, model = rows.shape
    scr = pltpu.VMEM((tokens, model), bf16)
    return call(
        functools.partial(finish_kernel, slots),
        [jax.ShapeDtypeStruct((tokens, model), bf16)] * 2,
        4 * slots.rows * tokens * model,
        6 * tokens * model + 2 * block.size,
        [VMEM] * 4 + [HBM],
        [HBM, HBM],
        [scr, scr, scr, pltpu.SemaphoreType.DMA((slots.cuts or 2, 2)), pltpu.SemaphoreType.DMA],
        limit=ALMOST_ALL,
    )(keys, kept, block, dec_bias, rows)


def shards(
    query_rows,
    key_rows,
    value_matrix,
    doc_ids,
    out_weight,
    enc_weight,
    enc_bias,
    dec_weight,
    dec_bias,
    expert_ids,
    slot_ids,
):
    q, k, v = query_rows[0], key_rows[0], value_matrix[0]
    tokens = q.shape[0]
    size, exp_size = lax.axis_size("seq"), lax.axis_size("exp")
    chips = size // CORES
    devices = size * exp_size
    me = lax.axis_index("seq")
    chip, core = me // CORES, me % CORES
    q_cols, kv_cols = q.shape[1] // chips, k.shape[1] // chips
    heads = q.shape[1] // k.shape[1]
    groups = kv_cols // HEAD_DIMENSION
    span = tokens * size
    model = out_weight.shape[1]
    cols = model // CHUNKS

    def over(d):
        return [
            (a * CORES + b, ((a + d) % chips) * CORES + b)
            for a in range(chips)
            for b in range(CORES)
        ]

    swap = [(a, a ^ 1) for a in range(size)]

    def cut(x, at, n):
        return lax.dynamic_slice(x, (0, at * n), (x.shape[0], n))

    pair = lambda at: jnp.concatenate([cut(k, at, kv_cols), cut(v, at, kv_cols)], axis=1)
    kv_parts, q_parts = [pair(chip)], [q]
    for d in range(1, chips):
        to = (chip + d) % chips
        kv_parts.append(lax.ppermute(pair(to), "seq", over(d)))
        q_parts.append(lax.ppermute(cut(q, to, q_cols), "seq", over(d)))
    mine = jnp.concatenate(kv_parts, axis=0)
    theirs = lax.ppermute(mine, "seq", swap)

    ring = [2 * i for i in range(exp_size // 2)] + [2 * i + 1 for i in reversed(range(exp_size // 2))]
    exp_me = lax.axis_index("exp")
    place = jnp.where(exp_me % 2 == 0, exp_me // 2, exp_size - 1 - exp_me // 2)
    offsets = [0]
    for step in range(1, exp_size // 2):
        offsets += [-step, step]
    offsets.append(exp_size // 2)
    spot = (place + jnp.array(offsets, jnp.int32)) % exp_size
    order = jnp.where(spot < exp_size // 2, 2 * spot, 2 * (exp_size - 1 - spot) + 1)
    deep = out_weight.shape[0]
    order = jnp.concatenate(
        [(c * exp_size + order) * deep for c in (core, 1 - core)]
    ).astype(jnp.int32)
    w_blocks = [
        ring_gather(out_weight[:, j * cols : (j + 1) * cols], ring, swap, j % 2 == 1)
        for j in range(CHUNKS)
    ]

    doc_col = jnp.concatenate([doc_ids, jnp.full((1, KEY_BLOCK), -1, jnp.int32)], axis=1)
    doc_row = doc_ids.reshape(span, 1)
    starts = jnp.sum(
        (doc_ids < doc_ids[0, ::ROW_BLOCK][:, None]).astype(jnp.int32), axis=1
    ) // KEY_STEP
    seats = jnp.stack(
        [
            ((chip - a) % chips) * CORES + c
            for a in range(chips)
            for c in (core, 1 - core)
        ]
    )
    attended = []
    for d in range(chips):
        lane = chip * q_cols if d == 0 else 0 * chip
        scal = jnp.concatenate([jnp.stack([seats[d * CORES], lane]), seats]).astype(jnp.int32)
        attended.append([])
        for g in range(groups):
            attended[d].append(
                attend(scal, starts, q_parts[d], heads, g, mine, theirs, doc_col, doc_row, chips)
            )

    capacity = 2 * tokens // devices
    slots = Slots(capacity, devices)
    keys = slot_keys(slots, expert_ids[0], slot_ids[0])
    kept = (slot_ids[0] >= 0).astype(jnp.int32).reshape(tokens, 1)
    bias_row = dec_bias[None]
    whole_rows = None
    arrived = []

    def to_all(block):
        return lax.all_to_all(
            block.reshape(devices, 8, block.shape[1]), ("seq", "exp"), 0, 0, tiled=True
        ).reshape(block.shape)

    for j in range(CHUNKS):
        w_all, *sends = project_far(order, *w_blocks[j], attended[1:])
        received = [
            lax.ppermute(part, "seq", over(chips - d)) for d, part in enumerate(sends, start=1)
        ]
        own = project_own(attended[0], w_all)
        packed, whole_rows = pack(slots, keys, own, received, whole_rows, j)
        arrived.append(to_all(packed))

    pre, arrived[0] = encode(slots, arrived[0], bias_row, enc_weight, cols)
    latent, packed, arrived[1] = middle(
        slots, arrived[1], bias_row, enc_bias, enc_weight, pre, dec_weight, model - cols
    )
    returned = to_all(packed)
    dec_grad = decoder_grad(slots, latent, packed, arrived, model)
    recon, error = finish(slots, keys, kept, returned, bias_row, whole_rows)
    return (whole_rows[None], recon[None], error[None], dec_grad)


def solution(mesh):
    return jax.shard_map(
        shards,
        mesh=mesh,
        in_specs=(
            P("exp", "seq", None),
            P("exp", "seq", None),
            P("exp", "seq", None),
            P("exp", None),
            P(("seq", "exp"), None),
            P(("seq", "exp"), None, None),
            P(("seq", "exp"), None),
            P(("seq", "exp"), None, None),
            P(),
            P("exp", "seq"),
            P("exp", "seq"),
        ),
        out_specs=(
            P("exp", "seq", None),
            P("exp", "seq", None),
            P("exp", "seq", None),
            P(("seq", "exp"), None, None),
        ),
        check_vma=False,
    )
```

```python
import functools
import math

import jax
import jax.numpy as jnp
from jax import lax
from jax.experimental import pallas as pl
from jax.experimental.pallas import tpu as pltpu
from jax.sharding import PartitionSpec as P


HEAD_DIMENSION = 128
CORES = 2
KEY_BLOCK = 256
KEY_STEP = 16
ROW_BLOCK = 64
EMPTY = 1e30
MASKED = -1e30
CHUNKS = 2
LIMIT = 20 * 2**20
VMEM, SMEM, ANY, HBM = pltpu.VMEM, pltpu.SMEM, pl.ANY, pltpu.HBM
TILES = 4

bf16 = jnp.bfloat16
f32 = jnp.float32


def call(kernel, out_shape, flops, moved, ins, outs, scratch=(), alias={}, limit=None):
    spec = lambda space: pl.BlockSpec(memory_space=space)
    return pl.pallas_call(
        kernel,
        out_shape=out_shape,
        in_specs=[spec(s) for s in ins],
        out_specs=jax.tree.map(spec, outs),
        scratch_shapes=list(scratch),
        input_output_aliases=alias,
        cost_estimate=pl.CostEstimate(flops=int(flops), bytes_accessed=int(moved), transcendentals=0),
        compiler_params=pltpu.CompilerParams(vmem_limit_bytes=limit or LIMIT),
    )


def in_hbm(x):
    return pltpu.with_memory_space_constraint(x, pltpu.HBM)


def dot(a, b, dims=((1,), (0,))):
    return lax.dot_general(a, b, (dims, ((), ())), preferred_element_type=f32)


def attention_kernel(
    heads, parts, group, scal, first, q_ref, mine_ref, theirs_ref, dcol_ref, drow_ref, o_ref,
    k_scr, v_scr, m_scr, l_scr, a_scr,
):
    tokens = q_ref.shape[0]
    hd = HEAD_DIMENSION
    width = mine_ref.shape[1] // 2
    span = parts * CORES * tokens
    key_at = slice(group * hd, (group + 1) * hd)
    value_at = slice(width + group * hd, width + (group + 1) * hd)
    for d in range(parts):
        for which, ref in enumerate((mine_ref, theirs_ref)):
            at = pl.multiple_of(scal[2 + d * CORES + which] * tokens, tokens)
            k_scr[pl.ds(at, tokens), :] = ref[d * tokens : (d + 1) * tokens, key_at]
            v_scr[pl.ds(at, tokens), :] = ref[d * tokens : (d + 1) * tokens, value_at]
    k_scr[span:, :] = jnp.zeros((KEY_BLOCK, hd), bf16)
    v_scr[span:, :] = jnp.zeros((KEY_BLOCK, hd), bf16)

    base = scal[0] * tokens
    scale = math.log2(math.e) / math.sqrt(hd)
    rows = heads * ROW_BLOCK
    blocks = tokens // ROW_BLOCK
    lane_pos = lax.broadcasted_iota(jnp.int32, (ROW_BLOCK, KEY_BLOCK), 1)
    row_in = lax.broadcasted_iota(jnp.int32, (ROW_BLOCK, KEY_BLOCK), 0)

    def queries(i):
        at = slice(i * ROW_BLOCK, (i + 1) * ROW_BLOCK)
        lane = [pl.multiple_of(scal[1] + (group * heads + h) * hd, hd) for h in range(heads)]
        return jnp.concatenate([q_ref[at, pl.ds(n, hd)] for n in lane], axis=0)

    def doc_starts(i):
        here = pl.multiple_of(base + i * ROW_BLOCK, ROW_BLOCK)
        earlier = dcol_ref[...] < drow_ref[pl.ds(here, ROW_BLOCK), :]
        return jnp.sum(earlier.astype(f32), axis=1, keepdims=True).astype(jnp.int32)

    def scores(i, q, col, begin):
        col = pl.multiple_of(col, KEY_STEP)
        s = dot(q, k_scr[pl.ds(col, KEY_BLOCK), :], ((1,), (1,))) * scale
        key_pos = lane_pos + col
        visible = (row_in + (base + i * ROW_BLOCK) >= key_pos) & (key_pos >= begin)
        s = jnp.where(visible[None], s.reshape(heads, ROW_BLOCK, KEY_BLOCK), MASKED)
        return s.reshape(rows, KEY_BLOCK)

    def values(col):
        return v_scr[pl.ds(pl.multiple_of(col, KEY_STEP), KEY_BLOCK), :]

    starts = [first[scal[0] * blocks + i] * KEY_STEP for i in range(blocks)]
    for i in range(blocks):
        s = scores(i, queries(i), starts[i], doc_starts(i))
        top = jnp.max(s, axis=1, keepdims=True)
        p = jnp.exp2(s - top)
        m_scr[i] = top
        l_scr[i] = jnp.sum(p, axis=1, keepdims=True)
        a_scr[i] = dot(p.astype(bf16), values(starts[i]))

    trips = 1
    for i in range(blocks):
        need = (base + (i + 1) * ROW_BLOCK - starts[i] + KEY_BLOCK - 1) // KEY_BLOCK
        trips = jnp.maximum(trips, need)

    def more(j, carry):
        for i in range(blocks):
            col = jnp.minimum(starts[i] + j * KEY_BLOCK, span)
            s = scores(i, queries(i), col, doc_starts(i))
            old = m_scr[i]
            top = jnp.maximum(old, jnp.max(s, axis=1, keepdims=True))
            p = jnp.exp2(s - top)
            fade = jnp.exp2(old - top)
            m_scr[i] = top
            l_scr[i] = l_scr[i] * fade + jnp.sum(p, axis=1, keepdims=True)
            a_scr[i] = a_scr[i] * fade + dot(p.astype(bf16), values(col))
        return carry

    lax.fori_loop(1, trips, more, 0)

    for i in range(blocks):
        out = (a_scr[i] * (1.0 / l_scr[i])).astype(bf16)
        for h in range(heads):
            o_ref[i * ROW_BLOCK : (i + 1) * ROW_BLOCK, h * hd : (h + 1) * hd] = out[
                h * ROW_BLOCK : (h + 1) * ROW_BLOCK
            ]


def attend(scal, first, q, heads, group, mine, theirs, doc_col, doc_row, parts):
    tokens = q.shape[0]
    span = parts * CORES * tokens
    rows = heads * ROW_BLOCK
    lanes = heads * HEAD_DIMENSION
    blocks = tokens // ROW_BLOCK
    keys = pltpu.VMEM((span + KEY_BLOCK, HEAD_DIMENSION), bf16)
    column = pltpu.VMEM((blocks, rows, 1), f32)
    return call(
        functools.partial(attention_kernel, heads, parts, group),
        jax.ShapeDtypeStruct((tokens, lanes), bf16),
        4 * tokens * lanes * span // 2,
        4 * tokens * lanes + 8 * span * HEAD_DIMENSION,
        [SMEM, SMEM] + [VMEM] * 5,
        VMEM,
        [keys, keys, column, column, pltpu.VMEM((blocks, rows, HEAD_DIMENSION), f32)],
    )(scal, first, q, mine, theirs, doc_col, doc_row)


def ring_gather(w, ring, swap, flip):
    size = len(ring)
    half = size // 2
    ahead = [(ring[i], ring[(i + 1) % size]) for i in range(size)]
    back = [(ring[i], ring[(i - 1) % size]) for i in range(size)]
    fw = bw = w
    blocks = [w]
    for step in range(1, half + 1):
        if step < half or not flip:
            fw = lax.ppermute(fw, "exp", ahead)
            blocks.append(fw)
        if step < half or flip:
            bw = lax.ppermute(bw, "exp", back)
            blocks.append(bw)
    theirs = [lax.ppermute(b, "seq", swap) for b in blocks]
    return blocks, theirs


def project_far_kernel(blocks, pieces, parts, order, *refs):
    w_refs, refs = refs[: 2 * blocks], refs[2 * blocks :]
    att, refs = refs[: parts * pieces], refs[parts * pieces :]
    w_out, sends = refs[0], refs[1:]
    for which in range(2):
        for i in range(blocks):
            ref = w_refs[which * blocks + i]
            n = ref.shape[0]
            at = pl.multiple_of(order[which * blocks + i], n)
            w_out[pl.ds(at, n), :] = ref[...]
    for d, send in enumerate(sends):
        x = jnp.concatenate([r[...] for r in att[d * pieces : (d + 1) * pieces]], axis=1)
        send[...] = dot(x, w_out[...]).astype(bf16)


def project_far(order, mine, theirs, attended):
    tokens = attended[0][0].shape[0]
    pieces = len(attended[0])
    width = sum(a.shape[1] for a in attended[0])
    cols = mine[0].shape[1]
    parts = len(attended)
    flat = [a for group in attended for a in group]
    return call(
        functools.partial(project_far_kernel, len(mine), pieces, parts),
        [jax.ShapeDtypeStruct((width, cols), bf16)]
        + [jax.ShapeDtypeStruct((tokens, cols), bf16)] * parts,
        2 * parts * tokens * width * cols,
        2 * parts * tokens * width + 4 * width * cols,
        [SMEM] + [VMEM] * (2 * len(mine) + len(flat)),
        [VMEM] * (1 + parts),
    )(order, *mine, *theirs, *flat)


def project_own_kernel(*refs):
    att, (w_ref, out_ref) = refs[:-2], refs[-2:]
    out_ref[...] = dot(jnp.concatenate([r[...] for r in att], axis=1), w_ref[...])


def project_own(attended, w):
    tokens = attended[0].shape[0]
    width, cols = w.shape
    return call(
        project_own_kernel,
        jax.ShapeDtypeStruct((tokens, cols), f32),
        2 * tokens * width * cols,
        2 * tokens * width + 2 * width * cols,
        [VMEM] * (len(attended) + 1),
        VMEM,
    )(*attended, w)


class Slots:
    def __init__(self, capacity, devices):
        self.full = capacity // 8
        rest = capacity % 8
        self.tail = 0
        if rest:
            self.tail = 1
            while self.tail < rest:
                self.tail *= 2
        self.cuts = 8 // self.tail if self.tail else 0
        self.rows = 8 * devices
        self.groups = self.full + (1 if self.tail else 0)

    def width(self, cols):
        return self.full * cols + (cols // self.cuts if self.tail else 0)


def slot_keys(slots, expert, slot):
    keys = []
    kept = slot >= 0
    for g in range(slots.full):
        ok = kept & (slot >= 8 * g) & (slot < 8 * g + 8)
        keys.append(jnp.where(ok, expert * 8 + slot - 8 * g, -1))
    if slots.tail:
        rest = slot - 8 * slots.full
        for i in range(slots.cuts):
            keys.append(jnp.where(kept & (rest >= 0), expert * 8 + i * slots.tail + rest, -1))
    return jnp.stack(keys, axis=0).astype(jnp.int32)


def one_hot(keys_ref, i, rows):
    n = keys_ref.shape[1]
    return lax.broadcasted_iota(jnp.int32, (rows, n), 0) == keys_ref[i : i + 1, :]


def send(group, cols, src, dst, sems):
    at = slice(group * cols, min((group + 1) * cols, src.shape[1]))
    copy = pltpu.make_async_copy(src.at[:, at], dst.at[:, at], sems.at[group])
    copy.start()
    return copy


def pack_kernel(slots, parts, chunk, keys_ref, own_ref, *refs):
    recv, (packed_ref, rows_ref, x_ref, out_ref, sem, out_sem) = refs[:parts], refs[-6:]
    total = own_ref[...]
    for r in recv:
        total = total + r[...].astype(f32)
    x = total.astype(bf16)
    x_ref[...] = x
    cols = x.shape[1]
    copy = pltpu.make_async_copy(x_ref, rows_ref.at[:, chunk * cols : (chunk + 1) * cols], sem)
    copy.start()

    sent = []

    def place(hot, part):
        hot = hot.astype(f32)
        return dot(hot.astype(bf16), part), jnp.sum(hot, axis=1, keepdims=True)

    for g in range(slots.full):
        rows, live = place(one_hot(keys_ref, g, slots.rows), x)
        out_ref[:, g * cols : (g + 1) * cols] = jnp.where(live > 0, rows, EMPTY).astype(bf16)
        sent.append(send(g, cols, out_ref, packed_ref, out_sem))
    if slots.tail:
        cut = cols // slots.cuts
        acc = live_all = None
        for i in range(slots.cuts):
            rows, live = place(one_hot(keys_ref, slots.full + i, slots.rows), x[:, i * cut : (i + 1) * cut])
            acc = rows if acc is None else acc + rows
            live_all = live if live_all is None else live_all + live
        out_ref[:, slots.full * cols :] = jnp.where(live_all > 0, acc, EMPTY).astype(bf16)
        sent.append(send(slots.full, cols, out_ref, packed_ref, out_sem))
    copy.wait()
    for part in sent:
        part.wait()


def pack(slots, keys, own, received, rows_out, chunk):
    tokens, cols = own.shape
    width = slots.width(cols)
    parts = len(received)
    args = [keys, own, *received]
    ins = [VMEM] * len(args)
    alias = {}
    if rows_out is not None:
        alias = {len(args): 1}
        args.append(rows_out)
        ins.append(ANY)
    return call(
        functools.partial(pack_kernel, slots, parts, chunk),
        [
            pltpu.HBM((slots.rows, width), bf16),
            jax.ShapeDtypeStruct((tokens, cols * CHUNKS), bf16),
        ],
        4 * slots.rows * tokens * cols,
        8 * tokens * cols + 2 * slots.rows * width,
        ins,
        [HBM, ANY],
        [
            pltpu.VMEM((tokens, cols), bf16),
            pltpu.VMEM((slots.rows, width), bf16),
            pltpu.SemaphoreType.DMA,
            pltpu.SemaphoreType.DMA((slots.groups,)),
        ],
        alias,
    )(*args)


def spread(slots, block):
    cols = block.shape[1]
    full, cuts = slots.full, slots.cuts
    n = cols * cuts // (full * cuts + 1) if slots.tail else cols // full
    out = [block[:, g * n : (g + 1) * n].astype(f32) for g in range(full)]
    if slots.tail:
        rest = block[:, full * n :].astype(f32)
        rows = rest.shape[0]
        out.append(
            jnp.concatenate(
                [rest]
                + [pltpu.roll(rest, rows - i * slots.tail, 0) for i in range(1, cuts)],
                axis=1,
            )
        )
    return out


def tail_rows(shape):
    return lax.broadcasted_iota(jnp.int32, shape, 0) % 8


def live_rows(slots, groups):
    out = []
    for g, rows in enumerate(groups):
        live = rows[:, :1] < EMPTY / 2
        if slots.tail and g == slots.full:
            live = live & (tail_rows(live.shape) < slots.tail)
        out.append(live)
    return out


def row_tiles(ref, scr, sems, start):
    n = scr.shape[0] // TILES
    copies = []
    for t in range(TILES):
        copies.append(
            pltpu.make_async_copy(
                ref.at[start + t * n : start + (t + 1) * n], scr.at[t * n : (t + 1) * n], sems.at[t]
            )
        )
        copies[-1].start()
    return copies


def centered_rows(slots, block_ref, bias):
    groups = spread(slots, block_ref[...])
    live = live_rows(slots, groups)
    rows = [jnp.where(a, r - bias, 0.0).astype(bf16) for a, r in zip(live, groups)]
    return jnp.concatenate(rows, axis=0), live


def encode_kernel(slots, block_ref, bias_ref, w_ref, out_ref, kept_ref, w_scr, sems, kept_sem):
    cols = w_scr.shape[0]
    copies = row_tiles(w_ref.at[0], w_scr, sems, 0)
    kept = pltpu.make_async_copy(block_ref, kept_ref, kept_sem)
    kept.start()
    x, _ = centered_rows(slots, block_ref, bias_ref[:, :cols])
    for copy in copies:
        copy.wait()
    out_ref[...] = dot(x, w_scr[...]).astype(bf16)
    kept.wait()


def encode(slots, block, dec_bias, enc, cols):
    hidden = enc.shape[2]
    n = slots.rows * slots.groups
    return call(
        functools.partial(encode_kernel, slots),
        [jax.ShapeDtypeStruct((n, hidden), bf16), pltpu.HBM(block.shape, bf16)],
        2 * n * cols * hidden,
        2 * cols * hidden + 2 * block.size + 4 * n * hidden,
        [VMEM, VMEM, HBM],
        [VMEM, HBM],
        [
            pltpu.VMEM((cols, hidden), bf16),
            pltpu.SemaphoreType.DMA((TILES,)),
            pltpu.SemaphoreType.DMA,
        ],
    )(block, dec_bias, in_hbm(enc))


def middle_kernel(
    slots, block_ref, bias_ref, enc_bias_ref, enc_ref, prev_ref, dec_ref,
    latent_out, packed_ref, kept_ref,
    e_scr, d_scr, p_scr, latent_scr, pack_scr, e_sems, d_sems, p_sem, kept_sem, latent_sem, sems,
):
    cols = e_scr.shape[0]
    _, model = d_scr.shape
    e_copies = row_tiles(enc_ref.at[0], e_scr, e_sems, model - cols)
    prev = pltpu.make_async_copy(prev_ref, p_scr, p_sem)
    prev.start()
    cuts = slots.cuts or 2
    cut = model // cuts
    d_copies = []
    for t in range(cuts):
        at = slice(t * cut, (t + 1) * cut)
        d_copies.append(
            pltpu.make_async_copy(dec_ref.at[0, :, at], d_scr.at[:, at], d_sems.at[t])
        )
        d_copies[-1].start()
    kept = pltpu.make_async_copy(block_ref, kept_ref, kept_sem)
    x, live = centered_rows(slots, block_ref, bias_ref[:, model - cols :])
    n = slots.rows
    for copy in e_copies:
        copy.wait()
    kept.start()
    prev.wait()
    total = dot(x, e_scr[...]) + p_scr[...].astype(f32) + enc_bias_ref[...]
    for g, a in enumerate(live):
        rows = slice(g * n, (g + 1) * n)
        pre = jnp.maximum(total[rows], 0.0)
        latent_scr[rows] = jnp.where(a, pre, 0.0).astype(bf16)
    latent = pltpu.make_async_copy(latent_scr, latent_out, latent_sem)
    latent.start()
    sent = []
    rest = None
    which = tail_rows((n, 1)) // slots.tail if slots.tail else None
    for t in range(cuts):
        at = slice(t * cut, (t + 1) * cut)
        d_copies[t].wait()
        out = dot(latent_scr[...], d_scr[:, at]) + bias_ref[:, at]
        for g in range(slots.full):
            here = slice(g * model + at.start, g * model + at.stop)
            pack_scr[:, here] = out[g * n : (g + 1) * n].astype(bf16)
            sent.append(
                pltpu.make_async_copy(
                    pack_scr.at[:, here], packed_ref.at[:, here], sems.at[len(sent)]
                )
            )
            sent[-1].start()
        if slots.tail:
            part = out[slots.full * n :]
            rest = part if t == 0 else jnp.where(which == t, pltpu.roll(part, t * slots.tail, 0), rest)
    if slots.tail:
        here = slice(slots.full * model, slots.full * model + cut)
        pack_scr[:, here] = rest.astype(bf16)
        sent.append(
            pltpu.make_async_copy(pack_scr.at[:, here], packed_ref.at[:, here], sems.at[len(sent)])
        )
        sent[-1].start()
    kept.wait()
    latent.wait()
    for one in sent:
        one.wait()


def middle(slots, block, dec_bias, enc_bias, enc, prev, dec, cols):
    _, model, hidden = enc.shape
    n = slots.rows * slots.groups
    out = (slots.rows, slots.width(model))
    one = pltpu.SemaphoreType.DMA
    cuts = slots.cuts or 2
    return call(
        functools.partial(middle_kernel, slots),
        [
            pltpu.HBM((n, hidden), bf16),
            pltpu.HBM(out, bf16),
            pltpu.HBM(block.shape, bf16),
        ],
        2 * n * (cols + model) * hidden,
        2 * (cols + model) * hidden + 6 * block.size + 6 * n * hidden,
        [VMEM] * 3 + [HBM] * 3,
        [HBM] * 3,
        [
            pltpu.VMEM((cols, hidden), bf16),
            pltpu.VMEM((hidden, model), bf16),
            pltpu.VMEM((n, hidden), bf16),
            pltpu.VMEM((n, hidden), bf16),
            pltpu.VMEM(out, bf16),
            pltpu.SemaphoreType.DMA((TILES,)),
            pltpu.SemaphoreType.DMA((cuts,)),
            one, one, one,
            pltpu.SemaphoreType.DMA((slots.full * cuts + 1,)),
        ],
    )(block, dec_bias, enc_bias, in_hbm(enc), in_hbm(prev), in_hbm(dec))


def grad_kernel(slots, latent_ref, built_ref, *refs):
    *arrived, out_ref, scr, sems = refs
    cols = scr.shape[2]
    built = spread(slots, built_ref[...])
    copies = []
    for j, block_ref in enumerate(arrived):
        at = slice(j * cols, (j + 1) * cols)
        groups = spread(slots, block_ref[...])
        residue = jnp.concatenate(
            [
                jnp.where(a, r[:, at] - rows, 0.0).astype(bf16)
                for a, r, rows in zip(live_rows(slots, groups), built, groups)
            ],
            axis=0,
        )
        scr[j] = dot(latent_ref[...], residue, ((0,), (0,))).astype(bf16)
        copies.append(pltpu.make_async_copy(scr.at[j], out_ref.at[0, :, at], sems.at[j]))
        copies[-1].start()
    for copy in copies:
        copy.wait()


def decoder_grad(slots, latent, rebuilt, arrived, model):
    n, hidden = latent.shape
    parts = len(arrived)
    return call(
        functools.partial(grad_kernel, slots),
        jax.ShapeDtypeStruct((1, hidden, model), bf16),
        2 * n * hidden * model,
        2 * hidden * model + 2 * n * (hidden + model),
        [VMEM] * (2 + parts),
        ANY,
        [pltpu.VMEM((parts, hidden, model // parts), bf16), pltpu.SemaphoreType.DMA((parts,))],
    )(latent, rebuilt, *arrived)


def finish_kernel(
    slots, keys_ref, kept_ref, block_ref, bias_ref, rows_ref, recon_out, error_out,
    recon_scr, error_scr, rows_scr, sems, rows_sem,
):
    came = pltpu.make_async_copy(rows_ref, rows_scr, rows_sem)
    came.start()
    model = rows_scr.shape[1]
    cuts = slots.cuts or 2
    cut = model // cuts
    hot = [
        one_hot(keys_ref, i, slots.rows).astype(f32).astype(bf16)
        for i in range(keys_ref.shape[0])
    ]
    turn = lambda i, part: dot(hot[i], part, ((0,), (0,)))
    copies = []
    for t in range(cuts):
        at = slice(t * cut, (t + 1) * cut)
        total = 0.0
        for g in range(slots.full):
            total = total + turn(g, block_ref[:, g * model + at.start : g * model + at.stop])
        if slots.tail:
            total = total + turn(slots.full + t, block_ref[:, slots.full * model :])
        recon = jnp.where(kept_ref[...] > 0, total, bias_ref[:, at]).astype(bf16)
        recon_scr[:, at] = recon
        if t == 0:
            came.wait()
        error_scr[:, at] = (recon.astype(f32) - rows_scr[:, at].astype(f32)).astype(bf16)
        for k, (scr, out) in enumerate(((recon_scr, recon_out), (error_scr, error_out))):
            copies.append(pltpu.make_async_copy(scr.at[:, at], out.at[:, at], sems.at[t, k]))
            copies[-1].start()
    for copy in copies:
        copy.wait()


def finish(slots, keys, kept, block, dec_bias, rows):
    tokens, model = rows.shape
    scr = pltpu.VMEM((tokens, model), bf16)
    return call(
        functools.partial(finish_kernel, slots),
        [jax.ShapeDtypeStruct((tokens, model), bf16)] * 2,
        4 * slots.rows * tokens * model,
        6 * tokens * model + 2 * block.size,
        [VMEM] * 4 + [HBM],
        [HBM, HBM],
        [scr, scr, scr, pltpu.SemaphoreType.DMA((slots.cuts or 2, 2)), pltpu.SemaphoreType.DMA],
    )(keys, kept, block, dec_bias, in_hbm(rows))


def shards(
    query_rows,
    key_rows,
    value_matrix,
    doc_ids,
    out_weight,
    enc_weight,
    enc_bias,
    dec_weight,
    dec_bias,
    expert_ids,
    slot_ids,
):
    q, k, v = query_rows[0], key_rows[0], value_matrix[0]
    tokens = q.shape[0]
    size, exp_size = lax.axis_size("seq"), lax.axis_size("exp")
    chips = size // CORES
    devices = size * exp_size
    me = lax.axis_index("seq")
    chip, core = me // CORES, me % CORES
    q_cols, kv_cols = q.shape[1] // chips, k.shape[1] // chips
    heads = q.shape[1] // k.shape[1]
    groups = kv_cols // HEAD_DIMENSION
    span = tokens * size
    model = out_weight.shape[1]
    cols = model // CHUNKS

    def over(d):
        return [
            (a * CORES + b, ((a + d) % chips) * CORES + b)
            for a in range(chips)
            for b in range(CORES)
        ]

    swap = [(a, a ^ 1) for a in range(size)]

    def cut(x, at, n):
        return lax.dynamic_slice(x, (0, at * n), (x.shape[0], n))

    pair = lambda at: jnp.concatenate([cut(k, at, kv_cols), cut(v, at, kv_cols)], axis=1)
    kv_parts, q_parts = [pair(chip)], [q]
    for d in range(1, chips):
        to = (chip + d) % chips
        kv_parts.append(lax.ppermute(pair(to), "seq", over(d)))
        q_parts.append(lax.ppermute(cut(q, to, q_cols), "seq", over(d)))
    mine = jnp.concatenate(kv_parts, axis=0)
    theirs = lax.ppermute(mine, "seq", swap)

    ring = [2 * i for i in range(exp_size // 2)] + [2 * i + 1 for i in reversed(range(exp_size // 2))]
    exp_me = lax.axis_index("exp")
    place = jnp.where(exp_me % 2 == 0, exp_me // 2, exp_size - 1 - exp_me // 2)
    offsets = [0]
    for step in range(1, exp_size // 2):
        offsets += [-step, step]
    offsets.append(exp_size // 2)
    spot = (place + jnp.array(offsets, jnp.int32)) % exp_size
    order = jnp.where(spot < exp_size // 2, 2 * spot, 2 * (exp_size - 1 - spot) + 1)
    deep = out_weight.shape[0]
    order = jnp.concatenate(
        [(c * exp_size + order) * deep for c in (core, 1 - core)]
    ).astype(jnp.int32)
    w_blocks = [
        ring_gather(out_weight[:, j * cols : (j + 1) * cols], ring, swap, j % 2 == 1)
        for j in range(CHUNKS)
    ]

    doc_col = doc_ids
    doc_row = doc_ids.reshape(span, 1)
    starts = jnp.sum(
        (doc_ids < doc_ids[0, ::ROW_BLOCK][:, None]).astype(jnp.int32), axis=1
    ) // KEY_STEP
    seats = jnp.stack(
        [
            ((chip - a) % chips) * CORES + c
            for a in range(chips)
            for c in (core, 1 - core)
        ]
    )
    attended = []
    for d in range(chips):
        lane = chip * q_cols if d == 0 else 0 * chip
        scal = jnp.concatenate([jnp.stack([seats[d * CORES], lane]), seats]).astype(jnp.int32)
        attended.append([])
        for g in range(groups):
            attended[d].append(
                attend(scal, starts, q_parts[d], heads, g, mine, theirs, doc_col, doc_row, chips)
            )

    capacity = 2 * tokens // devices
    slots = Slots(capacity, devices)
    keys = slot_keys(slots, expert_ids[0], slot_ids[0])
    kept = (slot_ids[0] >= 0).astype(jnp.int32).reshape(tokens, 1)
    bias_row = dec_bias[None]
    whole_rows = None
    arrived = []

    def to_all(block):
        return lax.all_to_all(
            block.reshape(devices, 8, block.shape[1]), ("seq", "exp"), 0, 0, tiled=True
        ).reshape(block.shape)

    for j in range(CHUNKS):
        w_all, *sends = project_far(order, *w_blocks[j], attended[1:])
        received = [
            lax.ppermute(part, "seq", over(chips - d)) for d, part in enumerate(sends, start=1)
        ]
        own = project_own(attended[0], w_all)
        packed, whole_rows = pack(slots, keys, own, received, whole_rows, j)
        arrived.append(to_all(packed))

    pre, arrived[0] = encode(slots, arrived[0], bias_row, enc_weight, cols)
    latent, packed, arrived[1] = middle(
        slots, arrived[1], bias_row, enc_bias, enc_weight, pre, dec_weight, model - cols
    )
    returned = to_all(packed)
    dec_grad = decoder_grad(slots, latent, packed, arrived, model)
    recon, error = finish(slots, keys, kept, returned, bias_row, whole_rows)
    return (whole_rows[None], recon[None], error[None], dec_grad)


def solution(mesh):
    return jax.shard_map(
        shards,
        mesh=mesh,
        in_specs=(
            P("exp", "seq", None),
            P("exp", "seq", None),
            P("exp", "seq", None),
            P("exp", None),
            P(("seq", "exp"), None),
            P(("seq", "exp"), None, None),
            P(("seq", "exp"), None),
            P(("seq", "exp"), None, None),
            P(),
            P("exp", "seq"),
            P("exp", "seq"),
        ),
        out_specs=(
            P("exp", "seq", None),
            P("exp", "seq", None),
            P("exp", "seq", None),
            P(("seq", "exp"), None, None),
        ),
        check_vma=False,
    )
```

```python
import functools
import math

import jax
import jax.numpy as jnp
from jax import lax
from jax.experimental import pallas as pl
from jax.experimental.pallas import tpu as pltpu
from jax.sharding import PartitionSpec as P


HEAD_DIMENSION = 128
CORES = 2
KEY_BLOCK = 256
KEY_STEP = 16
MORE_KEYS = 128
ROW_BLOCK = 64
EMPTY = 1e30
MASKED = -1e30
CHUNKS = 2
LIMIT = 20 * 2**20
VMEM, SMEM, ANY, HBM = pltpu.VMEM, pltpu.SMEM, pl.ANY, pltpu.HBM
TILES = 4

bf16 = jnp.bfloat16
f32 = jnp.float32


def call(kernel, out_shape, flops, moved, ins, outs, scratch=(), alias={}, limit=None):
    spec = lambda space: pl.BlockSpec(memory_space=space)
    return pl.pallas_call(
        kernel,
        out_shape=out_shape,
        in_specs=[spec(s) for s in ins],
        out_specs=jax.tree.map(spec, outs),
        scratch_shapes=list(scratch),
        input_output_aliases=alias,
        cost_estimate=pl.CostEstimate(flops=int(flops), bytes_accessed=int(moved), transcendentals=0),
        compiler_params=pltpu.CompilerParams(vmem_limit_bytes=limit or LIMIT),
    )


def in_hbm(x):
    return pltpu.with_memory_space_constraint(x, pltpu.HBM)


def dot(a, b, dims=((1,), (0,))):
    return lax.dot_general(a, b, (dims, ((), ())), preferred_element_type=f32)


def attention_kernel(
    heads, parts, group, scal, first, q_ref, mine_ref, theirs_ref, dcol_ref, drow_ref, o_ref,
    k_scr, v_scr, m_scr, l_scr, a_scr,
):
    tokens = q_ref.shape[0]
    hd = HEAD_DIMENSION
    width = mine_ref.shape[1] // 2
    span = parts * CORES * tokens
    key_at = slice(group * hd, (group + 1) * hd)
    value_at = slice(width + group * hd, width + (group + 1) * hd)
    for d in range(parts):
        for which, ref in enumerate((mine_ref, theirs_ref)):
            at = pl.multiple_of(scal[2 + d * CORES + which] * tokens, tokens)
            k_scr[pl.ds(at, tokens), :] = ref[d * tokens : (d + 1) * tokens, key_at]
            v_scr[pl.ds(at, tokens), :] = ref[d * tokens : (d + 1) * tokens, value_at]
    k_scr[span:, :] = jnp.zeros((KEY_BLOCK, hd), bf16)
    v_scr[span:, :] = jnp.zeros((KEY_BLOCK, hd), bf16)

    base = scal[0] * tokens
    scale = math.log2(math.e) / math.sqrt(hd)
    rows = heads * ROW_BLOCK
    blocks = tokens // ROW_BLOCK

    def queries(i):
        at = slice(i * ROW_BLOCK, (i + 1) * ROW_BLOCK)
        lane = [pl.multiple_of(scal[1] + (group * heads + h) * hd, hd) for h in range(heads)]
        return jnp.concatenate([q_ref[at, pl.ds(n, hd)] for n in lane], axis=0)

    def doc_starts(i):
        here = pl.multiple_of(base + i * ROW_BLOCK, ROW_BLOCK)
        earlier = dcol_ref[...] < drow_ref[pl.ds(here, ROW_BLOCK), :]
        return jnp.sum(earlier.astype(f32), axis=1, keepdims=True).astype(jnp.int32)

    def scores(i, q, col, begin, size):
        col = pl.multiple_of(col, KEY_STEP)
        s = dot(q, k_scr[pl.ds(col, size), :], ((1,), (1,))) * scale
        key_pos = lax.broadcasted_iota(jnp.int32, (ROW_BLOCK, size), 1) + col
        row_pos = lax.broadcasted_iota(jnp.int32, (ROW_BLOCK, size), 0) + (base + i * ROW_BLOCK)
        visible = (row_pos >= key_pos) & (key_pos >= begin)
        s = jnp.where(visible[None], s.reshape(heads, ROW_BLOCK, size), MASKED)
        return s.reshape(rows, size)

    def values(col, size):
        return v_scr[pl.ds(pl.multiple_of(col, KEY_STEP), size), :]

    starts = [first[scal[0] * blocks + i] * KEY_STEP for i in range(blocks)]
    for i in range(blocks):
        s = scores(i, queries(i), starts[i], doc_starts(i), KEY_BLOCK)
        top = jnp.max(s, axis=1, keepdims=True)
        p = jnp.exp2(s - top)
        m_scr[i] = top
        l_scr[i] = jnp.sum(p, axis=1, keepdims=True)
        a_scr[i] = dot(p.astype(bf16), values(starts[i], KEY_BLOCK))

    trips = 0
    for i in range(blocks):
        left = base + (i + 1) * ROW_BLOCK - starts[i] - KEY_BLOCK
        trips = jnp.maximum(trips, (left + MORE_KEYS - 1) // MORE_KEYS)

    def more(j, carry):
        for i in range(blocks):
            col = jnp.minimum(starts[i] + KEY_BLOCK + j * MORE_KEYS, span)
            s = scores(i, queries(i), col, doc_starts(i), MORE_KEYS)
            old = m_scr[i]
            top = jnp.maximum(old, jnp.max(s, axis=1, keepdims=True))
            p = jnp.exp2(s - top)
            fade = jnp.exp2(old - top)
            m_scr[i] = top
            l_scr[i] = l_scr[i] * fade + jnp.sum(p, axis=1, keepdims=True)
            a_scr[i] = a_scr[i] * fade + dot(p.astype(bf16), values(col, MORE_KEYS))
        return carry

    lax.fori_loop(0, trips, more, 0)

    for i in range(blocks):
        out = (a_scr[i] * (1.0 / l_scr[i])).astype(bf16)
        for h in range(heads):
            o_ref[i * ROW_BLOCK : (i + 1) * ROW_BLOCK, h * hd : (h + 1) * hd] = out[
                h * ROW_BLOCK : (h + 1) * ROW_BLOCK
            ]


def attend(scal, first, q, heads, group, mine, theirs, doc_col, doc_row, parts):
    tokens = q.shape[0]
    span = parts * CORES * tokens
    rows = heads * ROW_BLOCK
    lanes = heads * HEAD_DIMENSION
    blocks = tokens // ROW_BLOCK
    keys = pltpu.VMEM((span + KEY_BLOCK, HEAD_DIMENSION), bf16)
    column = pltpu.VMEM((blocks, rows, 1), f32)
    return call(
        functools.partial(attention_kernel, heads, parts, group),
        jax.ShapeDtypeStruct((tokens, lanes), bf16),
        4 * tokens * lanes * span // 2,
        4 * tokens * lanes + 8 * span * HEAD_DIMENSION,
        [SMEM, SMEM] + [VMEM] * 5,
        VMEM,
        [keys, keys, column, column, pltpu.VMEM((blocks, rows, HEAD_DIMENSION), f32)],
    )(scal, first, q, mine, theirs, doc_col, doc_row)


def ring_gather(w, ring, swap, flip):
    size = len(ring)
    half = size // 2
    ahead = [(ring[i], ring[(i + 1) % size]) for i in range(size)]
    back = [(ring[i], ring[(i - 1) % size]) for i in range(size)]
    fw = bw = w
    blocks = [w]
    for step in range(1, half + 1):
        if step < half or not flip:
            fw = lax.ppermute(fw, "exp", ahead)
            blocks.append(fw)
        if step < half or flip:
            bw = lax.ppermute(bw, "exp", back)
            blocks.append(bw)
    theirs = [lax.ppermute(b, "seq", swap) for b in blocks]
    return blocks, theirs


def project_far_kernel(blocks, pieces, parts, order, *refs):
    w_refs, refs = refs[: 2 * blocks], refs[2 * blocks :]
    att, refs = refs[: parts * pieces], refs[parts * pieces :]
    w_out, *sends, sem = refs
    depth = w_refs[0].shape[0]
    copies = []
    for i, ref in enumerate(w_refs):
        at = pl.multiple_of(order[i], depth)
        copies.append(pltpu.make_async_copy(ref, w_out.at[pl.ds(at, depth), :], sem.at[i]))
        copies[-1].start()
    x = [
        jnp.concatenate([r[...] for r in att[d * pieces : (d + 1) * pieces]], axis=1)
        for d in range(parts)
    ]
    for copy in copies:
        copy.wait()
    for d, send in enumerate(sends):
        send[...] = dot(x[d], w_out[...]).astype(bf16)


def project_far(order, mine, theirs, attended, hbm):
    tokens = attended[0][0].shape[0]
    pieces = len(attended[0])
    width = sum(a.shape[1] for a in attended[0])
    cols = mine[0].shape[1]
    parts = len(attended)
    flat = [a for group in attended for a in group]
    blocks = [*mine, *theirs]
    if hbm:
        blocks = [in_hbm(b) for b in blocks]
    return call(
        functools.partial(project_far_kernel, len(mine), pieces, parts),
        [jax.ShapeDtypeStruct((width, cols), bf16)]
        + [jax.ShapeDtypeStruct((tokens, cols), bf16)] * parts,
        2 * parts * tokens * width * cols,
        2 * parts * tokens * width + 4 * width * cols,
        [SMEM] + [HBM if hbm else VMEM] * len(blocks) + [VMEM] * len(flat),
        [VMEM] * (1 + parts),
        [pltpu.SemaphoreType.DMA((len(blocks),))],
    )(order, *blocks, *flat)


def project_own_kernel(*refs):
    att, (w_ref, out_ref) = refs[:-2], refs[-2:]
    out_ref[...] = dot(jnp.concatenate([r[...] for r in att], axis=1), w_ref[...])


def project_own(attended, w):
    tokens = attended[0].shape[0]
    width, cols = w.shape
    return call(
        project_own_kernel,
        jax.ShapeDtypeStruct((tokens, cols), f32),
        2 * tokens * width * cols,
        2 * tokens * width + 2 * width * cols,
        [VMEM] * (len(attended) + 1),
        VMEM,
    )(*attended, w)


class Slots:
    tail = 4
    cuts = 2

    def __init__(self, capacity, devices):
        self.full = capacity // 8
        rest = capacity % 8
        if rest > self.tail:
            self.full, rest = self.full + 1, 0
        self.has_tail = rest > 0
        self.rows = 8 * devices
        self.groups = self.full + self.has_tail
        self.lines = self.rows * self.full + (self.rows // 2 if self.has_tail else 0)

    def width(self, cols):
        return self.full * cols + (cols // self.cuts if self.has_tail else 0)


def slot_keys(slots, expert, slot):
    keys = []
    kept = slot >= 0
    for g in range(slots.full):
        ok = kept & (slot >= 8 * g) & (slot < 8 * g + 8)
        keys.append(jnp.where(ok, expert * 8 + slot - 8 * g, -1))
    if slots.has_tail:
        rest = slot - 8 * slots.full
        for i in range(slots.cuts):
            keys.append(jnp.where(kept & (rest >= 0), expert * 8 + i * slots.tail + rest, -1))
    return jnp.stack(keys, axis=0).astype(jnp.int32)


def one_hot(keys_ref, i, rows):
    n = keys_ref.shape[1]
    return lax.broadcasted_iota(jnp.int32, (rows, n), 0) == keys_ref[i : i + 1, :]


def send(group, cols, src, dst, sems):
    at = slice(group * cols, min((group + 1) * cols, src.shape[1]))
    copy = pltpu.make_async_copy(src.at[:, at], dst.at[:, at], sems.at[group])
    copy.start()
    return copy


def pack_kernel(slots, parts, chunk, keys_ref, own_ref, *refs):
    recv, (packed_ref, rows_ref, x_ref, out_ref, sem, out_sem) = refs[:parts], refs[-6:]
    total = own_ref[...]
    for r in recv:
        total = total + r[...].astype(f32)
    x = total.astype(bf16)
    x_ref[...] = x
    cols = x.shape[1]
    copy = pltpu.make_async_copy(x_ref, rows_ref.at[:, chunk * cols : (chunk + 1) * cols], sem)
    copy.start()

    sent = []

    def place(hot, part):
        hot = hot.astype(f32)
        return dot(hot.astype(bf16), part), jnp.sum(hot, axis=1, keepdims=True)

    for g in range(slots.full):
        rows, live = place(one_hot(keys_ref, g, slots.rows), x)
        out_ref[:, g * cols : (g + 1) * cols] = jnp.where(live > 0, rows, EMPTY).astype(bf16)
        sent.append(send(g, cols, out_ref, packed_ref, out_sem))
    if slots.has_tail:
        cut = cols // slots.cuts
        acc = live_all = None
        for i in range(slots.cuts):
            rows, live = place(one_hot(keys_ref, slots.full + i, slots.rows), x[:, i * cut : (i + 1) * cut])
            acc = rows if acc is None else acc + rows
            live_all = live if live_all is None else live_all + live
        out_ref[:, slots.full * cols :] = jnp.where(live_all > 0, acc, EMPTY).astype(bf16)
        sent.append(send(slots.full, cols, out_ref, packed_ref, out_sem))
    copy.wait()
    for part in sent:
        part.wait()


def pack(slots, keys, own, received, rows_out, chunk):
    tokens, cols = own.shape
    width = slots.width(cols)
    parts = len(received)
    args = [keys, own, *received]
    ins = [VMEM] * len(args)
    alias = {}
    if rows_out is not None:
        alias = {len(args): 1}
        args.append(rows_out)
        ins.append(ANY)
    return call(
        functools.partial(pack_kernel, slots, parts, chunk),
        [
            pltpu.HBM((slots.rows, width), bf16),
            jax.ShapeDtypeStruct((tokens, cols * CHUNKS), bf16),
        ],
        4 * slots.rows * tokens * cols,
        8 * tokens * cols + 2 * slots.rows * width,
        ins,
        [HBM, ANY],
        [
            pltpu.VMEM((tokens, cols), bf16),
            pltpu.VMEM((slots.rows, width), bf16),
            pltpu.SemaphoreType.DMA,
            pltpu.SemaphoreType.DMA((slots.groups,)),
        ],
        alias,
    )(*args)


def low_rows(shape):
    return lax.broadcasted_iota(jnp.int32, shape, 0) % 8 < 4


def by_pairs(x):
    rows, n = x.shape
    x = x.reshape(rows // 16, 2, 8, n)
    return x[:, 0].reshape(rows // 2, n), x[:, 1].reshape(rows // 2, n)


def turned(x):
    return pltpu.roll(x, 4, 0), pltpu.roll(x, x.shape[0] - 4, 0)


def spread(slots, block):
    cols = block.shape[1]
    full = slots.full
    n = cols * 2 // (full * 2 + 1) if slots.has_tail else cols // full
    out = [block[:, g * n : (g + 1) * n].astype(f32) for g in range(full)]
    if slots.has_tail:
        even, odd = by_pairs(block[:, full * n :].astype(f32))
        low = low_rows((even.shape[0], 1))
        out.append(
            jnp.concatenate(
                [jnp.where(low, even, turned(odd)[0]), jnp.where(low, turned(even)[1], odd)], axis=1
            )
        )
    return out


def gather_tail(halves):
    first, second = halves
    low = low_rows((first.shape[0], 1))
    even = jnp.where(low, first, turned(second)[0])
    odd = jnp.where(low, turned(first)[1], second)
    rows, n = first.shape
    pairs = [x.reshape(rows // 8, 1, 8, n) for x in (even, odd)]
    return jnp.concatenate(pairs, axis=1).reshape(2 * rows, n)


def live_rows(groups):
    return [rows[:, :1] < EMPTY / 2 for rows in groups]


def row_tiles(ref, scr, sems, start):
    n = scr.shape[0] // TILES
    copies = []
    for t in range(TILES):
        copies.append(
            pltpu.make_async_copy(
                ref.at[start + t * n : start + (t + 1) * n], scr.at[t * n : (t + 1) * n], sems.at[t]
            )
        )
        copies[-1].start()
    return copies


def centered_rows(slots, block_ref, bias):
    groups = spread(slots, block_ref[...])
    live = live_rows(groups)
    rows = [jnp.where(a, r - bias, 0.0).astype(bf16) for a, r in zip(live, groups)]
    return jnp.concatenate(rows, axis=0), live


def encode_kernel(slots, block_ref, bias_ref, w_ref, out_ref, kept_ref, w_scr, sems, kept_sem):
    cols = w_scr.shape[0]
    copies = row_tiles(w_ref.at[0], w_scr, sems, 0)
    kept = pltpu.make_async_copy(block_ref, kept_ref, kept_sem)
    kept.start()
    x, _ = centered_rows(slots, block_ref, bias_ref[:, :cols])
    for copy in copies:
        copy.wait()
    out_ref[...] = dot(x, w_scr[...]).astype(bf16)
    kept.wait()


def encode(slots, block, dec_bias, enc, cols):
    hidden = enc.shape[2]
    n = slots.lines
    return call(
        functools.partial(encode_kernel, slots),
        [jax.ShapeDtypeStruct((n, hidden), bf16), pltpu.HBM(block.shape, bf16)],
        2 * n * cols * hidden,
        2 * cols * hidden + 2 * block.size + 4 * n * hidden,
        [VMEM, VMEM, HBM],
        [VMEM, HBM],
        [
            pltpu.VMEM((cols, hidden), bf16),
            pltpu.SemaphoreType.DMA((TILES,)),
            pltpu.SemaphoreType.DMA,
        ],
    )(block, dec_bias, in_hbm(enc))


def middle_kernel(
    slots, block_ref, bias_ref, enc_bias_ref, enc_ref, prev_ref, dec_ref,
    latent_out, packed_ref, kept_ref,
    e_scr, d_scr, p_scr, latent_scr, pack_scr, e_sems, d_sems, p_sem, kept_sem, latent_sem, sems,
):
    cols = e_scr.shape[0]
    _, model = d_scr.shape
    e_copies = row_tiles(enc_ref.at[0], e_scr, e_sems, model - cols)
    prev = pltpu.make_async_copy(prev_ref, p_scr, p_sem)
    prev.start()
    cuts = slots.cuts
    cut = model // cuts
    d_copies = []
    for t in range(cuts):
        at = slice(t * cut, (t + 1) * cut)
        d_copies.append(
            pltpu.make_async_copy(dec_ref.at[0, :, at], d_scr.at[:, at], d_sems.at[t])
        )
    kept = pltpu.make_async_copy(block_ref, kept_ref, kept_sem)
    x, live = centered_rows(slots, block_ref, bias_ref[:, model - cols :])
    for copy in e_copies:
        copy.wait()
    for copy in d_copies:
        copy.start()
    kept.start()
    prev.wait()
    total = dot(x, e_scr[...]) + p_scr[...].astype(f32) + enc_bias_ref[...]
    at = 0
    for a in live:
        rows = slice(at, at + a.shape[0])
        latent_scr[rows] = jnp.where(a, jnp.maximum(total[rows], 0.0), 0.0).astype(bf16)
        at = rows.stop
    latent = pltpu.make_async_copy(latent_scr, latent_out, latent_sem)
    latent.start()
    sent = []
    n = slots.rows

    def go(here):
        sent.append(
            pltpu.make_async_copy(
                pack_scr.at[:, here], packed_ref.at[:, here], sems.at[len(sent)]
            )
        )
        sent[-1].start()

    halves = []
    for t in range(cuts):
        at = slice(t * cut, (t + 1) * cut)
        d_copies[t].wait()
        out = dot(latent_scr[...], d_scr[:, at]) + bias_ref[:, at]
        for g in range(slots.full):
            here = slice(g * model + at.start, g * model + at.stop)
            pack_scr[:, here] = out[g * n : (g + 1) * n].astype(bf16)
            go(here)
        halves.append(out[slots.full * n :])
    if slots.has_tail:
        here = slice(slots.full * model, slots.full * model + cut)
        pack_scr[:, here] = gather_tail(halves).astype(bf16)
        go(here)
    kept.wait()
    latent.wait()
    for one in sent:
        one.wait()


def middle(slots, block, dec_bias, enc_bias, enc, prev, dec, cols):
    _, model, hidden = enc.shape
    n = slots.lines
    out = (slots.rows, slots.width(model))
    one = pltpu.SemaphoreType.DMA
    cuts = slots.cuts
    return call(
        functools.partial(middle_kernel, slots),
        [
            pltpu.HBM((n, hidden), bf16),
            pltpu.HBM(out, bf16),
            pltpu.HBM(block.shape, bf16),
        ],
        2 * n * (cols + model) * hidden,
        2 * (cols + model) * hidden + 6 * block.size + 6 * n * hidden,
        [VMEM] * 3 + [HBM] * 3,
        [HBM] * 3,
        [
            pltpu.VMEM((cols, hidden), bf16),
            pltpu.VMEM((hidden, model), bf16),
            pltpu.VMEM((n, hidden), bf16),
            pltpu.VMEM((n, hidden), bf16),
            pltpu.VMEM(out, bf16),
            pltpu.SemaphoreType.DMA((TILES,)),
            pltpu.SemaphoreType.DMA((cuts,)),
            one, one, one,
            pltpu.SemaphoreType.DMA((slots.full * cuts + 1,)),
        ],
    )(block, dec_bias, enc_bias, in_hbm(enc), in_hbm(prev), in_hbm(dec))


def grad_kernel(slots, latent_ref, built_ref, *refs):
    *arrived, out_ref, scr, sems = refs
    cols = scr.shape[2]
    built = spread(slots, built_ref[...])
    copies = []
    for j, block_ref in enumerate(arrived):
        at = slice(j * cols, (j + 1) * cols)
        groups = spread(slots, block_ref[...])
        residue = jnp.concatenate(
            [
                jnp.where(a, r[:, at] - rows, 0.0).astype(bf16)
                for a, r, rows in zip(live_rows(groups), built, groups)
            ],
            axis=0,
        )
        scr[j] = dot(latent_ref[...], residue, ((0,), (0,))).astype(bf16)
        copies.append(pltpu.make_async_copy(scr.at[j], out_ref.at[0, :, at], sems.at[j]))
        copies[-1].start()
    for copy in copies:
        copy.wait()


def decoder_grad(slots, latent, rebuilt, arrived, model):
    n, hidden = latent.shape
    parts = len(arrived)
    return call(
        functools.partial(grad_kernel, slots),
        jax.ShapeDtypeStruct((1, hidden, model), bf16),
        2 * n * hidden * model,
        2 * hidden * model + 2 * n * (hidden + model),
        [VMEM] * (2 + parts),
        ANY,
        [pltpu.VMEM((parts, hidden, model // parts), bf16), pltpu.SemaphoreType.DMA((parts,))],
    )(latent, rebuilt, *arrived)


def finish_kernel(
    slots, keys_ref, kept_ref, block_ref, bias_ref, rows_ref, recon_out, error_out,
    recon_scr, error_scr, rows_scr, sems, rows_sem,
):
    came = pltpu.make_async_copy(rows_ref, rows_scr, rows_sem)
    came.start()
    model = rows_scr.shape[1]
    cuts = slots.cuts
    cut = model // cuts
    hot = [
        one_hot(keys_ref, i, slots.rows).astype(f32).astype(bf16)
        for i in range(keys_ref.shape[0])
    ]
    turn = lambda i, part: dot(hot[i], part, ((0,), (0,)))
    copies = []
    for t in range(cuts):
        at = slice(t * cut, (t + 1) * cut)
        total = 0.0
        for g in range(slots.full):
            total = total + turn(g, block_ref[:, g * model + at.start : g * model + at.stop])
        if slots.has_tail:
            total = total + turn(slots.full + t, block_ref[:, slots.full * model :])
        recon = jnp.where(kept_ref[...] > 0, total, bias_ref[:, at]).astype(bf16)
        recon_scr[:, at] = recon
        if t == 0:
            came.wait()
        error_scr[:, at] = (recon.astype(f32) - rows_scr[:, at].astype(f32)).astype(bf16)
        for k, (scr, out) in enumerate(((recon_scr, recon_out), (error_scr, error_out))):
            copies.append(pltpu.make_async_copy(scr.at[:, at], out.at[:, at], sems.at[t, k]))
            copies[-1].start()
    for copy in copies:
        copy.wait()


def finish(slots, keys, kept, block, dec_bias, rows):
    tokens, model = rows.shape
    scr = pltpu.VMEM((tokens, model), bf16)
    return call(
        functools.partial(finish_kernel, slots),
        [jax.ShapeDtypeStruct((tokens, model), bf16)] * 2,
        4 * slots.rows * tokens * model,
        6 * tokens * model + 2 * block.size,
        [VMEM] * 4 + [HBM],
        [HBM, HBM],
        [scr, scr, scr, pltpu.SemaphoreType.DMA((slots.cuts, 2)), pltpu.SemaphoreType.DMA],
    )(keys, kept, block, dec_bias, in_hbm(rows))


def shards(
    query_rows,
    key_rows,
    value_matrix,
    doc_ids,
    out_weight,
    enc_weight,
    enc_bias,
    dec_weight,
    dec_bias,
    expert_ids,
    slot_ids,
):
    q, k, v = query_rows[0], key_rows[0], value_matrix[0]
    tokens = q.shape[0]
    size, exp_size = lax.axis_size("seq"), lax.axis_size("exp")
    chips = size // CORES
    devices = size * exp_size
    me = lax.axis_index("seq")
    chip, core = me // CORES, me % CORES
    q_cols, kv_cols = q.shape[1] // chips, k.shape[1] // chips
    heads = q.shape[1] // k.shape[1]
    groups = kv_cols // HEAD_DIMENSION
    span = tokens * size
    model = out_weight.shape[1]
    cols = model // CHUNKS

    def over(d):
        return [
            (a * CORES + b, ((a + d) % chips) * CORES + b)
            for a in range(chips)
            for b in range(CORES)
        ]

    swap = [(a, a ^ 1) for a in range(size)]

    def cut(x, at, n):
        return lax.dynamic_slice(x, (0, at * n), (x.shape[0], n))

    pair = lambda at: jnp.concatenate([cut(k, at, kv_cols), cut(v, at, kv_cols)], axis=1)
    kv_parts, q_parts = [pair(chip)], [q]
    for d in range(1, chips):
        to = (chip + d) % chips
        kv_parts.append(lax.ppermute(pair(to), "seq", over(d)))
        q_parts.append(lax.ppermute(cut(q, to, q_cols), "seq", over(d)))
    mine = jnp.concatenate(kv_parts, axis=0)
    theirs = lax.ppermute(mine, "seq", swap)

    ring = [2 * i for i in range(exp_size // 2)] + [2 * i + 1 for i in reversed(range(exp_size // 2))]
    exp_me = lax.axis_index("exp")
    place = jnp.where(exp_me % 2 == 0, exp_me // 2, exp_size - 1 - exp_me // 2)
    offsets = [0]
    for step in range(1, exp_size // 2):
        offsets += [-step, step]
    offsets.append(exp_size // 2)
    spot = (place + jnp.array(offsets, jnp.int32)) % exp_size
    order = jnp.where(spot < exp_size // 2, 2 * spot, 2 * (exp_size - 1 - spot) + 1)
    deep = out_weight.shape[0]
    order = jnp.concatenate(
        [(c * exp_size + order) * deep for c in (core, 1 - core)]
    ).astype(jnp.int32)
    w_blocks = [
        ring_gather(out_weight[:, j * cols : (j + 1) * cols], ring, swap, j % 2 == 1)
        for j in range(CHUNKS)
    ]

    doc_col = doc_ids
    doc_row = doc_ids.reshape(span, 1)
    starts = jnp.sum(
        (doc_ids < doc_ids[0, ::ROW_BLOCK][:, None]).astype(jnp.int32), axis=1
    ) // KEY_STEP
    seats = jnp.stack(
        [
            ((chip - a) % chips) * CORES + c
            for a in range(chips)
            for c in (core, 1 - core)
        ]
    )
    attended = []
    for d in range(chips):
        lane = chip * q_cols if d == 0 else 0 * chip
        scal = jnp.concatenate([jnp.stack([seats[d * CORES], lane]), seats]).astype(jnp.int32)
        attended.append([])
        for g in range(groups):
            attended[d].append(
                attend(scal, starts, q_parts[d], heads, g, mine, theirs, doc_col, doc_row, chips)
            )

    capacity = 2 * tokens // devices
    slots = Slots(capacity, devices)
    keys = slot_keys(slots, expert_ids[0], slot_ids[0])
    kept = (slot_ids[0] >= 0).astype(jnp.int32).reshape(tokens, 1)
    bias_row = dec_bias[None]
    whole_rows = None
    arrived = []

    def to_all(block):
        return lax.all_to_all(
            block.reshape(devices, 8, block.shape[1]), ("seq", "exp"), 0, 0, tiled=True
        ).reshape(block.shape)

    for j in range(CHUNKS):
        w_all, *sends = project_far(order, *w_blocks[j], attended[1:], False)
        received = [
            lax.ppermute(part, "seq", over(chips - d)) for d, part in enumerate(sends, start=1)
        ]
        own = project_own(attended[0], w_all)
        packed, whole_rows = pack(slots, keys, own, received, whole_rows, j)
        arrived.append(to_all(packed))

    pre, arrived[0] = encode(slots, arrived[0], bias_row, enc_weight, cols)
    latent, packed, arrived[1] = middle(
        slots, arrived[1], bias_row, enc_bias, enc_weight, pre, dec_weight, model - cols
    )
    returned = to_all(packed)
    dec_grad = decoder_grad(slots, latent, packed, arrived, model)
    recon, error = finish(slots, keys, kept, returned, bias_row, whole_rows)
    return (whole_rows[None], recon[None], error[None], dec_grad)


def solution(mesh):
    return jax.shard_map(
        shards,
        mesh=mesh,
        in_specs=(
            P("exp", "seq", None),
            P("exp", "seq", None),
            P("exp", "seq", None),
            P("exp", None),
            P(("seq", "exp"), None),
            P(("seq", "exp"), None, None),
            P(("seq", "exp"), None),
            P(("seq", "exp"), None, None),
            P(),
            P("exp", "seq"),
            P("exp", "seq"),
        ),
        out_specs=(
            P("exp", "seq", None),
            P("exp", "seq", None),
            P("exp", "seq", None),
            P(("seq", "exp"), None, None),
        ),
        check_vma=False,
    )
```

```python
import functools
import math

import jax
import jax.numpy as jnp
from jax import lax
from jax.experimental import pallas as pl
from jax.experimental.pallas import tpu as pltpu
from jax.sharding import PartitionSpec as P


HEAD_DIMENSION = 128
CORES = 2
KEY_BLOCK = 256
KEY_STEP = 16
MORE_KEYS = 128
ROW_BLOCK = 64
EMPTY = 1e30
MASKED = -1e30
CHUNKS = 2
LIMIT = 20 * 2**20
VMEM, SMEM, ANY, HBM = pltpu.VMEM, pltpu.SMEM, pl.ANY, pltpu.HBM
TILES = 4

bf16 = jnp.bfloat16
f32 = jnp.float32


def call(kernel, out_shape, flops, moved, ins, outs, scratch=(), alias={}, limit=None):
    spec = lambda space: pl.BlockSpec(memory_space=space)
    return pl.pallas_call(
        kernel,
        out_shape=out_shape,
        in_specs=[spec(s) for s in ins],
        out_specs=jax.tree.map(spec, outs),
        scratch_shapes=list(scratch),
        input_output_aliases=alias,
        cost_estimate=pl.CostEstimate(flops=int(flops), bytes_accessed=int(moved), transcendentals=0),
        compiler_params=pltpu.CompilerParams(vmem_limit_bytes=limit or LIMIT),
    )


def in_hbm(x):
    return pltpu.with_memory_space_constraint(x, pltpu.HBM)


def dot(a, b, dims=((1,), (0,))):
    return lax.dot_general(a, b, (dims, ((), ())), preferred_element_type=f32)


def attention_kernel(
    heads, parts, group, scal, first, q_ref, mine_ref, theirs_ref, dcol_ref, drow_ref, o_ref,
    k_scr, v_scr, m_scr, l_scr, a_scr,
):
    tokens = q_ref.shape[0]
    hd = HEAD_DIMENSION
    width = mine_ref.shape[1] // 2
    span = parts * CORES * tokens
    key_at = slice(group * hd, (group + 1) * hd)
    value_at = slice(width + group * hd, width + (group + 1) * hd)
    for d in range(parts):
        for which, ref in enumerate((mine_ref, theirs_ref)):
            at = pl.multiple_of(scal[2 + d * CORES + which] * tokens, tokens)
            k_scr[pl.ds(at, tokens), :] = ref[d * tokens : (d + 1) * tokens, key_at]
            v_scr[pl.ds(at, tokens), :] = ref[d * tokens : (d + 1) * tokens, value_at]
    k_scr[span:, :] = jnp.zeros((KEY_BLOCK, hd), bf16)
    v_scr[span:, :] = jnp.zeros((KEY_BLOCK, hd), bf16)

    base = scal[0] * tokens
    scale = math.log2(math.e) / math.sqrt(hd)
    rows = heads * ROW_BLOCK
    blocks = tokens // ROW_BLOCK

    def queries(i):
        at = slice(i * ROW_BLOCK, (i + 1) * ROW_BLOCK)
        lane = [pl.multiple_of(scal[1] + (group * heads + h) * hd, hd) for h in range(heads)]
        return jnp.concatenate([q_ref[at, pl.ds(n, hd)] for n in lane], axis=0)

    def doc_starts(i):
        here = pl.multiple_of(base + i * ROW_BLOCK, ROW_BLOCK)
        earlier = dcol_ref[...] < drow_ref[pl.ds(here, ROW_BLOCK), :]
        return jnp.sum(earlier.astype(f32), axis=1, keepdims=True).astype(jnp.int32)

    def scores(i, q, col, begin, size):
        col = pl.multiple_of(col, KEY_STEP)
        s = dot(q, k_scr[pl.ds(col, size), :], ((1,), (1,))) * scale
        key_pos = lax.broadcasted_iota(jnp.int32, (ROW_BLOCK, size), 1) + col
        row_pos = lax.broadcasted_iota(jnp.int32, (ROW_BLOCK, size), 0) + (base + i * ROW_BLOCK)
        visible = (row_pos >= key_pos) & (key_pos >= begin)
        s = jnp.where(visible[None], s.reshape(heads, ROW_BLOCK, size), MASKED)
        return s.reshape(rows, size)

    def values(col, size):
        return v_scr[pl.ds(pl.multiple_of(col, KEY_STEP), size), :]

    starts = [first[scal[0] * blocks + i] * KEY_STEP for i in range(blocks)]
    for i in range(blocks):
        s = scores(i, queries(i), starts[i], doc_starts(i), KEY_BLOCK)
        top = jnp.max(s, axis=1, keepdims=True)
        p = jnp.exp2(s - top)
        m_scr[i] = top
        l_scr[i] = jnp.sum(p, axis=1, keepdims=True)
        a_scr[i] = dot(p.astype(bf16), values(starts[i], KEY_BLOCK))

    trips = 0
    for i in range(blocks):
        left = base + (i + 1) * ROW_BLOCK - starts[i] - KEY_BLOCK
        trips = jnp.maximum(trips, (left + MORE_KEYS - 1) // MORE_KEYS)

    def more(j, carry):
        for i in range(blocks):
            col = jnp.minimum(starts[i] + KEY_BLOCK + j * MORE_KEYS, span)
            s = scores(i, queries(i), col, doc_starts(i), MORE_KEYS)
            old = m_scr[i]
            top = jnp.maximum(old, jnp.max(s, axis=1, keepdims=True))
            p = jnp.exp2(s - top)
            fade = jnp.exp2(old - top)
            m_scr[i] = top
            l_scr[i] = l_scr[i] * fade + jnp.sum(p, axis=1, keepdims=True)
            a_scr[i] = a_scr[i] * fade + dot(p.astype(bf16), values(col, MORE_KEYS))
        return carry

    lax.fori_loop(0, trips, more, 0)

    for i in range(blocks):
        out = (a_scr[i] * (1.0 / l_scr[i])).astype(bf16)
        for h in range(heads):
            o_ref[i * ROW_BLOCK : (i + 1) * ROW_BLOCK, h * hd : (h + 1) * hd] = out[
                h * ROW_BLOCK : (h + 1) * ROW_BLOCK
            ]


def attend(scal, first, q, heads, group, mine, theirs, doc_col, doc_row, parts):
    tokens = q.shape[0]
    span = parts * CORES * tokens
    rows = heads * ROW_BLOCK
    lanes = heads * HEAD_DIMENSION
    blocks = tokens // ROW_BLOCK
    keys = pltpu.VMEM((span + KEY_BLOCK, HEAD_DIMENSION), bf16)
    column = pltpu.VMEM((blocks, rows, 1), f32)
    return call(
        functools.partial(attention_kernel, heads, parts, group),
        jax.ShapeDtypeStruct((tokens, lanes), bf16),
        4 * tokens * lanes * span // 2,
        4 * tokens * lanes + 8 * span * HEAD_DIMENSION,
        [SMEM, SMEM] + [VMEM] * 5,
        VMEM,
        [keys, keys, column, column, pltpu.VMEM((blocks, rows, HEAD_DIMENSION), f32)],
    )(scal, first, q, mine, theirs, doc_col, doc_row)


def ring_gather(w, ring, swap, flip):
    size = len(ring)
    half = size // 2
    ahead = [(ring[i], ring[(i + 1) % size]) for i in range(size)]
    back = [(ring[i], ring[(i - 1) % size]) for i in range(size)]
    fw = bw = w
    blocks = [w]
    for step in range(1, half + 1):
        if step < half or not flip:
            fw = lax.ppermute(fw, "exp", ahead)
            blocks.append(fw)
        if step < half or flip:
            bw = lax.ppermute(bw, "exp", back)
            blocks.append(bw)
    theirs = [lax.ppermute(b, "seq", swap) for b in blocks]
    return blocks, theirs


def project_far_kernel(blocks, pieces, parts, order, *refs):
    w_refs, refs = refs[: 2 * blocks], refs[2 * blocks :]
    att, refs = refs[: parts * pieces], refs[parts * pieces :]
    w_out, *sends, sem = refs
    depth = w_refs[0].shape[0]
    copies = []
    for i, ref in enumerate(w_refs):
        at = pl.multiple_of(order[i], depth)
        copies.append(pltpu.make_async_copy(ref, w_out.at[pl.ds(at, depth), :], sem.at[i]))
        copies[-1].start()
    x = [
        jnp.concatenate([r[...] for r in att[d * pieces : (d + 1) * pieces]], axis=1)
        for d in range(parts)
    ]
    for copy in copies:
        copy.wait()
    for d, send in enumerate(sends):
        send[...] = dot(x[d], w_out[...]).astype(bf16)


def project_far(order, mine, theirs, attended, hbm):
    tokens = attended[0][0].shape[0]
    pieces = len(attended[0])
    width = sum(a.shape[1] for a in attended[0])
    cols = mine[0].shape[1]
    parts = len(attended)
    flat = [a for group in attended for a in group]
    blocks = [*mine, *theirs]
    if hbm:
        blocks = [in_hbm(b) for b in blocks]
    return call(
        functools.partial(project_far_kernel, len(mine), pieces, parts),
        [jax.ShapeDtypeStruct((width, cols), bf16)]
        + [jax.ShapeDtypeStruct((tokens, cols), bf16)] * parts,
        2 * parts * tokens * width * cols,
        2 * parts * tokens * width + 4 * width * cols,
        [SMEM] + [HBM if hbm else VMEM] * len(blocks) + [VMEM] * len(flat),
        [VMEM] * (1 + parts),
        [pltpu.SemaphoreType.DMA((len(blocks),))],
    )(order, *blocks, *flat)


def project_own_kernel(*refs):
    att, (w_ref, out_ref) = refs[:-2], refs[-2:]
    out_ref[...] = dot(jnp.concatenate([r[...] for r in att], axis=1), w_ref[...])


def project_own(attended, w):
    tokens = attended[0].shape[0]
    width, cols = w.shape
    return call(
        project_own_kernel,
        jax.ShapeDtypeStruct((tokens, cols), f32),
        2 * tokens * width * cols,
        2 * tokens * width + 2 * width * cols,
        [VMEM] * (len(attended) + 1),
        VMEM,
    )(*attended, w)


class Slots:
    tail = 4
    cuts = 2

    def __init__(self, capacity, devices):
        self.full = capacity // 8
        rest = capacity % 8
        if rest > self.tail:
            self.full, rest = self.full + 1, 0
        self.has_tail = rest > 0
        self.rows = 8 * devices
        self.groups = self.full + self.has_tail
        self.lines = self.rows * self.full + (self.rows // 2 if self.has_tail else 0)

    def width(self, cols):
        return self.full * cols + (cols // self.cuts if self.has_tail else 0)


def slot_keys(slots, expert, slot):
    keys = []
    kept = slot >= 0
    for g in range(slots.full):
        ok = kept & (slot >= 8 * g) & (slot < 8 * g + 8)
        keys.append(jnp.where(ok, expert * 8 + slot - 8 * g, -1))
    if slots.has_tail:
        rest = slot - 8 * slots.full
        for i in range(slots.cuts):
            keys.append(jnp.where(kept & (rest >= 0), expert * 8 + i * slots.tail + rest, -1))
    return jnp.stack(keys, axis=0).astype(jnp.int32)


def one_hot(keys_ref, i, rows):
    n = keys_ref.shape[1]
    return lax.broadcasted_iota(jnp.int32, (rows, n), 0) == keys_ref[i : i + 1, :]


def send(group, cols, src, dst, sems):
    at = slice(group * cols, min((group + 1) * cols, src.shape[1]))
    copy = pltpu.make_async_copy(src.at[:, at], dst.at[:, at], sems.at[group])
    copy.start()
    return copy


def pack_kernel(slots, parts, chunk, keys_ref, own_ref, *refs):
    recv, (packed_ref, rows_ref, x_ref, out_ref, sem, out_sem) = refs[:parts], refs[-6:]
    total = own_ref[...]
    for r in recv:
        total = total + r[...].astype(f32)
    x = total.astype(bf16)
    x_ref[...] = x
    cols = x.shape[1]
    copy = pltpu.make_async_copy(x_ref, rows_ref.at[:, chunk * cols : (chunk + 1) * cols], sem)
    copy.start()

    sent = []

    def place(hot, part):
        hot = hot.astype(f32)
        return dot(hot.astype(bf16), part), jnp.sum(hot, axis=1, keepdims=True)

    for g in range(slots.full):
        rows, live = place(one_hot(keys_ref, g, slots.rows), x)
        out_ref[:, g * cols : (g + 1) * cols] = jnp.where(live > 0, rows, EMPTY).astype(bf16)
        sent.append(send(g, cols, out_ref, packed_ref, out_sem))
    if slots.has_tail:
        cut = cols // slots.cuts
        acc = live_all = None
        for i in range(slots.cuts):
            rows, live = place(one_hot(keys_ref, slots.full + i, slots.rows), x[:, i * cut : (i + 1) * cut])
            acc = rows if acc is None else acc + rows
            live_all = live if live_all is None else live_all + live
        out_ref[:, slots.full * cols :] = jnp.where(live_all > 0, acc, EMPTY).astype(bf16)
        sent.append(send(slots.full, cols, out_ref, packed_ref, out_sem))
    copy.wait()
    for part in sent:
        part.wait()


def pack(slots, keys, own, received, rows_out, chunk):
    tokens, cols = own.shape
    width = slots.width(cols)
    parts = len(received)
    args = [keys, own, *received]
    ins = [VMEM] * len(args)
    alias = {}
    if rows_out is not None:
        alias = {len(args): 1}
        args.append(rows_out)
        ins.append(ANY)
    return call(
        functools.partial(pack_kernel, slots, parts, chunk),
        [
            pltpu.HBM((slots.rows, width), bf16),
            jax.ShapeDtypeStruct((tokens, cols * CHUNKS), bf16),
        ],
        4 * slots.rows * tokens * cols,
        8 * tokens * cols + 2 * slots.rows * width,
        ins,
        [HBM, ANY],
        [
            pltpu.VMEM((tokens, cols), bf16),
            pltpu.VMEM((slots.rows, width), bf16),
            pltpu.SemaphoreType.DMA,
            pltpu.SemaphoreType.DMA((slots.groups,)),
        ],
        alias,
    )(*args)


def low_rows(shape):
    return lax.broadcasted_iota(jnp.int32, shape, 0) % 8 < 4


def by_pairs(x):
    rows, n = x.shape
    x = x.reshape(rows // 16, 2, 8, n)
    return x[:, 0].reshape(rows // 2, n), x[:, 1].reshape(rows // 2, n)


def turned(x):
    return pltpu.roll(x, 4, 0), pltpu.roll(x, x.shape[0] - 4, 0)


def spread(slots, block):
    cols = block.shape[1]
    full = slots.full
    n = cols * 2 // (full * 2 + 1) if slots.has_tail else cols // full
    out = [block[:, g * n : (g + 1) * n].astype(f32) for g in range(full)]
    if slots.has_tail:
        even, odd = by_pairs(block[:, full * n :].astype(f32))
        low = low_rows((even.shape[0], 1))
        out.append(
            jnp.concatenate(
                [jnp.where(low, even, turned(odd)[0]), jnp.where(low, turned(even)[1], odd)], axis=1
            )
        )
    return out


def gather_tail(halves):
    first, second = halves
    low = low_rows((first.shape[0], 1))
    even = jnp.where(low, first, turned(second)[0])
    odd = jnp.where(low, turned(first)[1], second)
    rows, n = first.shape
    pairs = [x.reshape(rows // 8, 1, 8, n) for x in (even, odd)]
    return jnp.concatenate(pairs, axis=1).reshape(2 * rows, n)


def live_rows(groups):
    return [rows[:, :1] < EMPTY / 2 for rows in groups]


def row_tiles(ref, scr, sems, start):
    n = scr.shape[0] // TILES
    copies = []
    for t in range(TILES):
        copies.append(
            pltpu.make_async_copy(
                ref.at[start + t * n : start + (t + 1) * n], scr.at[t * n : (t + 1) * n], sems.at[t]
            )
        )
        copies[-1].start()
    return copies


def centered_rows(slots, block_ref, bias):
    groups = spread(slots, block_ref[...])
    live = live_rows(groups)
    rows = [jnp.where(a, r - bias, 0.0).astype(bf16) for a, r in zip(live, groups)]
    return jnp.concatenate(rows, axis=0), live


def encode_kernel(slots, block_ref, bias_ref, w_ref, out_ref, kept_ref, w_scr, sems, kept_sem):
    cols = w_scr.shape[0]
    copies = row_tiles(w_ref.at[0], w_scr, sems, 0)
    kept = pltpu.make_async_copy(block_ref, kept_ref, kept_sem)
    kept.start()
    x, _ = centered_rows(slots, block_ref, bias_ref[:, :cols])
    for copy in copies:
        copy.wait()
    out_ref[...] = dot(x, w_scr[...]).astype(bf16)
    kept.wait()


def encode(slots, block, dec_bias, enc, cols):
    hidden = enc.shape[2]
    n = slots.lines
    return call(
        functools.partial(encode_kernel, slots),
        [jax.ShapeDtypeStruct((n, hidden), bf16), pltpu.HBM(block.shape, bf16)],
        2 * n * cols * hidden,
        2 * cols * hidden + 2 * block.size + 4 * n * hidden,
        [VMEM, VMEM, HBM],
        [VMEM, HBM],
        [
            pltpu.VMEM((cols, hidden), bf16),
            pltpu.SemaphoreType.DMA((TILES,)),
            pltpu.SemaphoreType.DMA,
        ],
    )(block, dec_bias, in_hbm(enc))


def middle_kernel(
    slots, block_ref, bias_ref, enc_bias_ref, enc_ref, prev_ref, dec_ref,
    latent_out, packed_ref, kept_ref,
    e_scr, d_scr, p_scr, latent_scr, pack_scr, e_sems, d_sems, p_sem, kept_sem, latent_sem, sems,
):
    cols = e_scr.shape[0]
    _, model = d_scr.shape
    e_copies = row_tiles(enc_ref.at[0], e_scr, e_sems, model - cols)
    prev = pltpu.make_async_copy(prev_ref, p_scr, p_sem)
    prev.start()
    tile = model // TILES
    d_copies = []
    for t in range(TILES):
        at = slice(t * tile, (t + 1) * tile)
        d_copies.append(
            pltpu.make_async_copy(dec_ref.at[0, :, at], d_scr.at[:, at], d_sems.at[t])
        )
    kept = pltpu.make_async_copy(block_ref, kept_ref, kept_sem)
    x, live = centered_rows(slots, block_ref, bias_ref[:, model - cols :])
    total = enc_bias_ref[...]
    deep = cols // TILES
    for t, copy in enumerate(e_copies):
        copy.wait()
        if t == 0:
            for later in d_copies:
                later.start()
        at = slice(t * deep, (t + 1) * deep)
        total = total + dot(x[:, at], e_scr[at])
    kept.start()
    prev.wait()
    total = total + p_scr[...].astype(f32)
    at = 0
    for a in live:
        rows = slice(at, at + a.shape[0])
        latent_scr[rows] = jnp.where(a, jnp.maximum(total[rows], 0.0), 0.0).astype(bf16)
        at = rows.stop
    latent = pltpu.make_async_copy(latent_scr, latent_out, latent_sem)
    latent.start()
    sent = []
    n = slots.rows

    def go(here):
        sent.append(
            pltpu.make_async_copy(
                pack_scr.at[:, here], packed_ref.at[:, here], sems.at[len(sent)]
            )
        )
        sent[-1].start()

    rest = []
    for t in range(TILES):
        at = slice(t * tile, (t + 1) * tile)
        d_copies[t].wait()
        out = dot(latent_scr[...], d_scr[:, at]) + bias_ref[:, at]
        for g in range(slots.full):
            here = slice(g * model + at.start, g * model + at.stop)
            pack_scr[:, here] = out[g * n : (g + 1) * n].astype(bf16)
            go(here)
        rest.append(out[slots.full * n :])
    if slots.has_tail:
        half = TILES // slots.cuts
        for t in range(half):
            at = slots.full * model + t * tile
            here = slice(at, at + tile)
            pack_scr[:, here] = gather_tail((rest[t], rest[half + t])).astype(bf16)
            go(here)
    kept.wait()
    latent.wait()
    for one in sent:
        one.wait()


def middle(slots, block, dec_bias, enc_bias, enc, prev, dec, cols):
    _, model, hidden = enc.shape
    n = slots.lines
    out = (slots.rows, slots.width(model))
    one = pltpu.SemaphoreType.DMA
    return call(
        functools.partial(middle_kernel, slots),
        [
            pltpu.HBM((n, hidden), bf16),
            pltpu.HBM(out, bf16),
            pltpu.HBM(block.shape, bf16),
        ],
        2 * n * (cols + model) * hidden,
        2 * (cols + model) * hidden + 6 * block.size + 6 * n * hidden,
        [VMEM] * 3 + [HBM] * 3,
        [HBM] * 3,
        [
            pltpu.VMEM((cols, hidden), bf16),
            pltpu.VMEM((hidden, model), bf16),
            pltpu.VMEM((n, hidden), bf16),
            pltpu.VMEM((n, hidden), bf16),
            pltpu.VMEM(out, bf16),
            pltpu.SemaphoreType.DMA((TILES,)),
            pltpu.SemaphoreType.DMA((TILES,)),
            one, one, one,
            pltpu.SemaphoreType.DMA((slots.full * TILES + TILES,)),
        ],
    )(block, dec_bias, enc_bias, in_hbm(enc), in_hbm(prev), in_hbm(dec))


def grad_kernel(slots, latent_ref, built_ref, *refs):
    *arrived, out_ref, scr, sems = refs
    cols = scr.shape[2]
    built = spread(slots, built_ref[...])
    copies = []
    for j, block_ref in enumerate(arrived):
        at = slice(j * cols, (j + 1) * cols)
        groups = spread(slots, block_ref[...])
        residue = jnp.concatenate(
            [
                jnp.where(a, r[:, at] - rows, 0.0).astype(bf16)
                for a, r, rows in zip(live_rows(groups), built, groups)
            ],
            axis=0,
        )
        scr[j] = dot(latent_ref[...], residue, ((0,), (0,))).astype(bf16)
        copies.append(pltpu.make_async_copy(scr.at[j], out_ref.at[0, :, at], sems.at[j]))
        copies[-1].start()
    for copy in copies:
        copy.wait()


def decoder_grad(slots, latent, rebuilt, arrived, model):
    n, hidden = latent.shape
    parts = len(arrived)
    return call(
        functools.partial(grad_kernel, slots),
        jax.ShapeDtypeStruct((1, hidden, model), bf16),
        2 * n * hidden * model,
        2 * hidden * model + 2 * n * (hidden + model),
        [VMEM] * (2 + parts),
        ANY,
        [pltpu.VMEM((parts, hidden, model // parts), bf16), pltpu.SemaphoreType.DMA((parts,))],
    )(latent, rebuilt, *arrived)


def finish_kernel(
    slots, keys_ref, kept_ref, block_ref, bias_ref, rows_ref, recon_out, error_out,
    recon_scr, error_scr, rows_scr, sems, rows_sem,
):
    came = pltpu.make_async_copy(rows_ref, rows_scr, rows_sem)
    came.start()
    model = rows_scr.shape[1]
    tile = model // TILES
    half = TILES // slots.cuts
    hot = [
        one_hot(keys_ref, i, slots.rows).astype(f32).astype(bf16)
        for i in range(keys_ref.shape[0])
    ]
    turn = lambda i, part: dot(hot[i], part, ((0,), (0,)))
    copies = []
    for t in range(TILES):
        at = slice(t * tile, (t + 1) * tile)
        total = 0.0
        for g in range(slots.full):
            total = total + turn(g, block_ref[:, g * model + at.start : g * model + at.stop])
        if slots.has_tail:
            here = slots.full * model + t % half * tile
            total = total + turn(slots.full + t // half, block_ref[:, here : here + tile])
        recon = jnp.where(kept_ref[...] > 0, total, bias_ref[:, at]).astype(bf16)
        recon_scr[:, at] = recon
        if t == 0:
            came.wait()
        error_scr[:, at] = (recon.astype(f32) - rows_scr[:, at].astype(f32)).astype(bf16)
        for k, (scr, out) in enumerate(((recon_scr, recon_out), (error_scr, error_out))):
            copies.append(pltpu.make_async_copy(scr.at[:, at], out.at[:, at], sems.at[t, k]))
            copies[-1].start()
    for copy in copies:
        copy.wait()


def finish(slots, keys, kept, block, dec_bias, rows):
    tokens, model = rows.shape
    scr = pltpu.VMEM((tokens, model), bf16)
    return call(
        functools.partial(finish_kernel, slots),
        [jax.ShapeDtypeStruct((tokens, model), bf16)] * 2,
        4 * slots.rows * tokens * model,
        6 * tokens * model + 2 * block.size,
        [VMEM] * 4 + [HBM],
        [HBM, HBM],
        [scr, scr, scr, pltpu.SemaphoreType.DMA((TILES, 2)), pltpu.SemaphoreType.DMA],
    )(keys, kept, block, dec_bias, in_hbm(rows))


def shards(
    query_rows,
    key_rows,
    value_matrix,
    doc_ids,
    out_weight,
    enc_weight,
    enc_bias,
    dec_weight,
    dec_bias,
    expert_ids,
    slot_ids,
):
    q, k, v = query_rows[0], key_rows[0], value_matrix[0]
    tokens = q.shape[0]
    size, exp_size = lax.axis_size("seq"), lax.axis_size("exp")
    chips = size // CORES
    devices = size * exp_size
    me = lax.axis_index("seq")
    chip, core = me // CORES, me % CORES
    q_cols, kv_cols = q.shape[1] // chips, k.shape[1] // chips
    heads = q.shape[1] // k.shape[1]
    groups = kv_cols // HEAD_DIMENSION
    span = tokens * size
    model = out_weight.shape[1]
    cols = model // CHUNKS

    def over(d):
        return [
            (a * CORES + b, ((a + d) % chips) * CORES + b)
            for a in range(chips)
            for b in range(CORES)
        ]

    swap = [(a, a ^ 1) for a in range(size)]

    def cut(x, at, n):
        return lax.dynamic_slice(x, (0, at * n), (x.shape[0], n))

    pair = lambda at: jnp.concatenate([cut(k, at, kv_cols), cut(v, at, kv_cols)], axis=1)
    kv_parts, q_parts = [pair(chip)], [q]
    for d in range(1, chips):
        to = (chip + d) % chips
        kv_parts.append(lax.ppermute(pair(to), "seq", over(d)))
        q_parts.append(lax.ppermute(cut(q, to, q_cols), "seq", over(d)))
    mine = jnp.concatenate(kv_parts, axis=0)
    theirs = lax.ppermute(mine, "seq", swap)

    ring = [2 * i for i in range(exp_size // 2)] + [2 * i + 1 for i in reversed(range(exp_size // 2))]
    exp_me = lax.axis_index("exp")
    place = jnp.where(exp_me % 2 == 0, exp_me // 2, exp_size - 1 - exp_me // 2)
    offsets = [0]
    for step in range(1, exp_size // 2):
        offsets += [-step, step]
    offsets.append(exp_size // 2)
    spot = (place + jnp.array(offsets, jnp.int32)) % exp_size
    order = jnp.where(spot < exp_size // 2, 2 * spot, 2 * (exp_size - 1 - spot) + 1)
    deep = out_weight.shape[0]
    order = jnp.concatenate(
        [(c * exp_size + order) * deep for c in (core, 1 - core)]
    ).astype(jnp.int32)
    w_blocks = [
        ring_gather(out_weight[:, j * cols : (j + 1) * cols], ring, swap, j % 2 == 1)
        for j in range(CHUNKS)
    ]

    doc_col = doc_ids
    doc_row = doc_ids.reshape(span, 1)
    starts = jnp.sum(
        (doc_ids < doc_ids[0, ::ROW_BLOCK][:, None]).astype(jnp.int32), axis=1
    ) // KEY_STEP
    seats = jnp.stack(
        [
            ((chip - a) % chips) * CORES + c
            for a in range(chips)
            for c in (core, 1 - core)
        ]
    )
    attended = []
    for d in range(chips):
        lane = chip * q_cols if d == 0 else 0 * chip
        scal = jnp.concatenate([jnp.stack([seats[d * CORES], lane]), seats]).astype(jnp.int32)
        attended.append([])
        for g in range(groups):
            attended[d].append(
                attend(scal, starts, q_parts[d], heads, g, mine, theirs, doc_col, doc_row, chips)
            )

    capacity = 2 * tokens // devices
    slots = Slots(capacity, devices)
    keys = slot_keys(slots, expert_ids[0], slot_ids[0])
    kept = (slot_ids[0] >= 0).astype(jnp.int32).reshape(tokens, 1)
    bias_row = dec_bias[None]
    whole_rows = None
    arrived = []

    def to_all(block):
        return lax.all_to_all(
            block.reshape(devices, 8, block.shape[1]), ("seq", "exp"), 0, 0, tiled=True
        ).reshape(block.shape)

    for j in range(CHUNKS):
        w_all, *sends = project_far(order, *w_blocks[j], attended[1:], False)
        received = [
            lax.ppermute(part, "seq", over(chips - d)) for d, part in enumerate(sends, start=1)
        ]
        own = project_own(attended[0], w_all)
        packed, whole_rows = pack(slots, keys, own, received, whole_rows, j)
        arrived.append(to_all(packed))

    pre, arrived[0] = encode(slots, arrived[0], bias_row, enc_weight, cols)
    latent, packed, arrived[1] = middle(
        slots, arrived[1], bias_row, enc_bias, enc_weight, pre, dec_weight, model - cols
    )
    returned = to_all(packed)
    dec_grad = decoder_grad(slots, latent, packed, arrived, model)
    recon, error = finish(slots, keys, kept, returned, bias_row, whole_rows)
    return (whole_rows[None], recon[None], error[None], dec_grad)


def solution(mesh):
    return jax.shard_map(
        shards,
        mesh=mesh,
        in_specs=(
            P("exp", "seq", None),
            P("exp", "seq", None),
            P("exp", "seq", None),
            P("exp", None),
            P(("seq", "exp"), None),
            P(("seq", "exp"), None, None),
            P(("seq", "exp"), None),
            P(("seq", "exp"), None, None),
            P(),
            P("exp", "seq"),
            P("exp", "seq"),
        ),
        out_specs=(
            P("exp", "seq", None),
            P("exp", "seq", None),
            P("exp", "seq", None),
            P(("seq", "exp"), None, None),
        ),
        check_vma=False,
    )
```
